32 devices in a mesh: shard: 4 (over x, core), rep: 8 (over z, y).
Axes of the slice: x: 2, y: 2, z: 4, core: 2. Of those that a mesh axis runs over, the one named last changes fastest.
Arguments:
- hidden_in: bfloat16 [32, 256, 2048], P(('shard', 'rep')), may hold values from -6 to 6
- segments: int32 [32, 256], P(('shard', 'rep')), may hold values from 0 to 7, never falling along the last dimension, each value on 1 to 128 neighbouring positions
- cotangent: bfloat16 [32, 256, 2048], P(('shard', 'rep')), may hold values from -6 to 6
- attn_gain: bfloat16 [2048], P('shard'), may hold values from 0.5 to 1.5
- w_query: bfloat16 [2048, 2048], P('shard'), may hold values from -0.125 to 0.125
- w_key: bfloat16 [2048, 256], P('shard'), may hold values from -0.125 to 0.125
- w_value: bfloat16 [2048, 256], P('shard'), may hold values from -0.125 to 0.125
- w_out: bfloat16 [2048, 2048], P('shard'), may hold values from -0.5 to 0.5
- mlp_gain: bfloat16 [2048], P('shard'), may hold values from 0.5 to 1.5
- w_gate: bfloat16 [2048, 5632], P('shard'), may hold values from -0.125 to 0.125
- w_up: bfloat16 [2048, 5632], P('shard'), may hold values from -0.125 to 0.125
- w_down: bfloat16 [5632, 2048], P('shard'), may hold values from -0.078125 to 0.078125
Outputs:
- layer_out: bfloat16 [32, 256, 2048], P(('shard', 'rep'))
- input_grad: float32 [32, 256, 2048], P(('shard', 'rep'))
- grad_attn_gain: float32 [2048], P('shard')
- grad_query: float32 [2048, 2048], P('shard')
- grad_key: float32 [2048, 256], P('shard')
- grad_value: float32 [2048, 256], P('shard')
- grad_out: float32 [2048, 2048], P('shard')
- grad_mlp_gain: float32 [2048], P('shard')
- grad_gate: float32 [2048, 5632], P('shard')
- grad_up: float32 [2048, 5632], P('shard')
- grad_down: float32 [5632, 2048], P('shard')
The draws below stay inside these ranges and needn't reach their ends.
Inputs may be any that keep to these rules, and one draw needn't show every extreme that they name: `segments`: segment numbers never fall along a sequence; a document holds at most 128 tokens, and some document holds exactly that many.
All inputs are finite; a program needn't handle non-finite values.
Results may differ from the reference program's by a relative error of at most 0.015.
Values may be sent and summed in bfloat16 or wider, within the bound.
A program may use at most 448 MiB of HBM per device.

```python
import math
import jax
import jax.numpy as jnp
import numpy as np
from jax import lax

D = 2048
HEADS = 32
KV_HEADS = 4
HEAD_DIM = 64
FF = 5632
SEQ = 256
DOCS = 8
DOC_MOST = 128
SEQS = 32


def block_scale(rng, extent, split, smallest, largest):
    gain, own = 1.0, jax.random.fold_in(rng, 6)
    for dim, shards_of in split:
        heights = jnp.exp(jax.random.uniform(jax.random.fold_in(own, dim), (shards_of,), jnp.float32, smallest / len(split), largest / len(split)))
        gain = gain * jnp.repeat(heights, extent[dim] // shards_of).reshape([-1 if axis == dim else 1 for axis in range(len(extent))])
    return gain


def length_profile(amount, total, bound, slope):
    weights = [(1 << 20) // math.isqrt(rank ** slope) + 1 for rank in range(2, amount + 1)]
    rest, holding = total - bound - (amount - 1), [1] * (amount - 1)
    while rest > 0:
        candidates = [i for i in range(amount - 1) if holding[i] < bound]
        whole, left = sum([weights[i] for i in candidates]), rest
        for i in candidates:
            extra = min(bound - holding[i], max(1, left * weights[i] // whole), rest)
            holding[i] = holding[i] + extra
            rest = rest - extra
    return np.array([bound] + holding)


def uneven_parts(own_key, count, total, most, slope):
    if count == 2:
        one = jax.random.randint(own_key, (), max(1, total - most), min(most, total - 1) + 1)
        return jnp.stack([one, total - one])
    lengths = jnp.asarray(length_profile(count, total, most, slope), jnp.int32)
    twos = (count - 1) // 2
    giver, sink = lengths[1:1 + 2 * twos:2], lengths[2:2 + 2 * twos:2]
    room = jnp.minimum(giver - 1, most - sink)
    shifted = jax.random.randint(jax.random.fold_in(own_key, 1), (twos,), 0, 1 << 20) % (room + 1)
    lengths = lengths.at[1:1 + 2 * twos:2].set(giver - shifted).at[2:2 + 2 * twos:2].set(sink + shifted)
    return lengths[jax.random.permutation(jax.random.fold_in(own_key, 2), count)]


def noise(stream_key, dims, deviation, reach, pieces=(), kind=jnp.bfloat16):
    values = jax.random.normal(stream_key, dims, jnp.float32) * deviation
    if len(pieces) > 0:
        values = block_scale(stream_key, dims, pieces, -0.22, 0.18) * values
    return jnp.clip(values, min=-reach, max=reach).astype(kind)


def setup_inputs(seed: int = 0) -> dict:
    splits = jax.random.split(jax.random.key(seed), 13)
    hidden_in = noise(splits[0], (SEQS, SEQ, D), 1.0, 6.0, ((0, 32),))
    segments = jax.vmap(lambda own: jnp.searchsorted(jnp.cumsum(uneven_parts(own, DOCS, SEQ, DOC_MOST, 0)), jnp.arange(SEQ), side="right"))(jax.random.split(splits[1], SEQS)).reshape((SEQS, SEQ)).astype(jnp.int32)
    cotangent = noise(splits[2], (SEQS, SEQ, D), 1.0, 6.0, ((0, 32),))
    attn_gain = jnp.clip(1.0 + 0.1 * jax.random.normal(splits[3], (D,), jnp.float32), 0.5, 1.5).astype(jnp.bfloat16)
    w_query = noise(splits[4], (D, D), D ** -0.5, 0.125, ((0, 4),))
    w_key = noise(splits[5], (D, KV_HEADS * HEAD_DIM), D ** -0.5, 0.125, ((0, 4),))
    w_value = noise(splits[6], (D, KV_HEADS * HEAD_DIM), D ** -0.5, 0.125, ((0, 4),))
    w_out = noise(splits[7], (D, D), (D // 16) ** -0.5, 0.5, ((0, 4),))
    mlp_gain = jnp.clip(1.0 + 0.1 * jax.random.normal(splits[8], (D,), jnp.float32), 0.5, 1.5).astype(jnp.bfloat16)
    w_gate = noise(splits[9], (D, FF), D ** -0.5, 0.125, ((0, 4),))
    w_up = noise(splits[10], (D, FF), D ** -0.5, 0.125, ((0, 4),))
    w_down = noise(splits[11], (FF, D), FF ** -0.5, 0.078125, ((0, 4),))
    return dict(hidden_in=hidden_in, segments=segments, cotangent=cotangent, attn_gain=attn_gain, w_query=w_query, w_key=w_key, w_value=w_value, w_out=w_out, mlp_gain=mlp_gain, w_gate=w_gate, w_up=w_up, w_down=w_down)


EPS = 1e-05
HIGHEST = lax.Precision.HIGHEST

@jax.custom_vjp
def low(v):
    return lax.optimization_barrier(v.astype(jnp.bfloat16)).astype(jnp.float32)

@jax.custom_vjp
def low_back(v):
    return v

def low_keep(v):
    return (low(v), None)

def low_pass(kept, grad):
    return (grad,)

def back_keep(v):
    return (v, None)

def back_low(kept, grad):
    return (low(grad),)
low.defvjp(low_keep, low_pass)
low_back.defvjp(back_keep, back_low)

def angles(segment_ids):
    length = segment_ids.shape[0]
    before = lax.optimization_barrier(jnp.sum((segment_ids[None, :] < segment_ids[:, None]).astype(jnp.int32), axis=1))
    place = (jnp.arange(length, dtype=jnp.int32) - before).astype(jnp.float32)
    half = HEAD_DIM // 2
    freqs = 10000.0 ** (-jnp.arange(half, dtype=jnp.float32) / half)
    turn = place[:, None] * freqs[None, :]
    return (jnp.cos(turn), jnp.sin(turn))

def rotate(values, cosine, sine):
    half = values.shape[-1] // 2
    first = values[..., :half]
    second = values[..., half:]
    cosine = cosine[:, None, :]
    sine = sine[:, None, :]
    return jnp.concatenate([first * cosine - second * sine, second * cosine + first * sine], axis=-1)

def matmul(left, right):
    return jnp.dot(left, right, precision=HIGHEST)

def layer(hidden, segment_ids, attn_gain, w_query, w_key, w_value, w_out, mlp_gain, w_gate, w_up, w_down):
    length = hidden.shape[0]
    group = HEADS // KV_HEADS
    factor = 1.0 / math.sqrt(HEAD_DIM)
    cosine, sine = angles(segment_ids)
    order = jnp.arange(length, dtype=jnp.int32)
    allowed = (segment_ids[:, None] == segment_ids[None, :]) & (order[:, None] >= order[None, :])
    scale1 = lax.rsqrt(lax.optimization_barrier(jnp.mean(hidden * hidden, axis=1, keepdims=True)) + EPS)
    normed1 = low(hidden * scale1 * attn_gain)
    query_raw = low_back(matmul(normed1, w_query))
    key_raw = low_back(matmul(normed1, w_key))
    values = low(low_back(matmul(normed1, w_value))).reshape(length, KV_HEADS, HEAD_DIM)
    query = low(rotate(query_raw.reshape(length, HEADS, HEAD_DIM), cosine, sine))
    keys = low(rotate(key_raw.reshape(length, KV_HEADS, HEAD_DIM), cosine, sine))
    grouped = query.reshape(length, KV_HEADS, group, HEAD_DIM)
    scores = low_back(jnp.einsum('qjgd,kjd->jgqk', grouped, keys, precision=HIGHEST) * factor)
    masked = jnp.where(allowed[None, None], scores, -1000000000.0)
    probs = low(jax.nn.softmax(masked, axis=-1))
    mixed = jnp.einsum('jgqk,kjd->qjgd', probs, values, precision=HIGHEST).reshape(length, HEADS * HEAD_DIM)
    attended = low(low_back(mixed))
    middle = hidden + low_back(matmul(attended, w_out))
    scale2 = lax.rsqrt(lax.optimization_barrier(jnp.mean(middle * middle, axis=1, keepdims=True)) + EPS)
    normed2 = low(middle * scale2 * mlp_gain)
    gate = low_back(matmul(normed2, w_gate))
    upward = low_back(matmul(normed2, w_up))
    inner = low(jax.nn.silu(gate) * upward)
    return middle + low_back(matmul(inner, w_down))

def reference(hidden_in, segments, cotangent, attn_gain, w_query, w_key, w_value, w_out, mlp_gain, w_gate, w_up, w_down):
    params = tuple((p.astype(jnp.float32) for p in (attn_gain, w_query, w_key, w_value, w_out, mlp_gain, w_gate, w_up, w_down)))

    def single(totals, item):
        hidden, segment_ids, upstream = item

        def forward(inputs, *weights):
            return layer(inputs, segment_ids, *weights)
        result, pullback = jax.vjp(forward, hidden.astype(jnp.float32), *params)
        grads = pullback(upstream.astype(jnp.float32))
        totals = tuple((t + g for t, g in zip(totals, grads[1:])))
        return (totals, (result.astype(jnp.bfloat16), grads[0]))
    zeros = tuple((jnp.zeros(p.shape, jnp.float32) for p in params))
    totals, (outputs, input_grads) = lax.scan(single, zeros, (hidden_in, segments, cotangent))
    return (outputs, input_grads, totals[0], totals[1], totals[2], totals[3], totals[4], totals[5], totals[6], totals[7], totals[8])
```

```python
import math

import jax
import jax.numpy as jnp
from jax import lax
from jax.sharding import PartitionSpec as P

HEADS = 32
KV_HEADS = 4
HEAD_DIM = 64
EPS = 1e-05
LOW = jnp.bfloat16
WIDE = jnp.float32


def mm(left, right):
    return jnp.dot(left, right, preferred_element_type=WIDE)


def contract_rows(left, right):
    return lax.dot_general(
        left, right, (((0,), (0,)), ((), ())), preferred_element_type=WIDE
    )


def contract_cols(left, right):
    return lax.dot_general(
        left, right, (((1,), (1,)), ((), ())), preferred_element_type=WIDE
    )


def angles(segment_ids):
    length = segment_ids.shape[-1]
    before = jnp.sum(
        (segment_ids[:, None, :] < segment_ids[:, :, None]).astype(jnp.int32), axis=2
    )
    place = (jnp.arange(length, dtype=jnp.int32)[None] - before).astype(WIDE)
    half = HEAD_DIM // 2
    freqs = 10000.0 ** (-jnp.arange(half, dtype=WIDE) / half)
    turn = place[..., None] * freqs
    return (jnp.cos(turn), jnp.sin(turn))


def rotate(values, cosine, sine):
    half = values.shape[-1] // 2
    first = values[..., :half]
    second = values[..., half:]
    return jnp.concatenate(
        [first * cosine - second * sine, second * cosine + first * sine], axis=-1
    )


def norm_back(normed_grad, gain, unit, scale):
    scaled = normed_grad * gain[None, :]
    return scale * (scaled - unit * jnp.mean(scaled * unit, axis=1, keepdims=True))


class Ring:
    def __init__(self, mesh):
        self.shards = mesh.shape["shard"]
        self.reps = mesh.shape["rep"]
        self.line = self.reps // 2
        self.shard = lax.axis_index("shard")
        self.rep = lax.axis_index("rep")
        self.low = self.rep % 2
        self.high = self.rep // 2
        self.side = (self.high >= self.line // 2).astype(jnp.int32)

    def swap(self, value, k):
        return lax.ppermute(value, "shard", [(s, s ^ k) for s in range(self.shards)])

    def pair(self, value):
        return lax.ppermute(value, "rep", [(r, r ^ 1) for r in range(self.reps)])

    def mid_pair(self, value):
        h = self.line // 2
        pairs = [(2 * z + y, (2 * z + y) ^ 1) for z in (h - 1, h) for y in (0, 1)]
        return lax.ppermute(value, "rep", pairs)

    def along(self, value, hops):
        pairs = [(2 * a + y, 2 * b + y) for a, b in hops for y in (0, 1)]
        return lax.ppermute(value, "rep", pairs)

    def inward(self, value):
        n = self.line
        for j in range(n // 2 - 1):
            value = value + self.along(value, [(j, j + 1), (n - 1 - j, n - 2 - j)])
        return value

    def across(self, value):
        h = self.line // 2
        return self.along(value, [(h - 1, h), (h, h - 1)])

    def outward(self, value):
        n = self.line
        for j in range(n // 2 - 2, -1, -1):
            got = self.along(value, [(j + 1, j), (n - 2 - j, n - 1 - j)])
            here = (self.high == j) | (self.high == n - 1 - j)
            value = jnp.where(here, got, value)
        return value

    def gather(self, own):
        far = self.swap(own, 2)
        return [own, self.swap(own, 1), far, self.swap(far, 1)]

    def scatter(self, blocks):
        near = self.swap(jnp.concatenate([blocks[1], blocks[3]], axis=0), 1)
        n = blocks[0].shape[0]
        far = blocks[2] + near[n:]
        return blocks[0] + near[:n], self.swap(far, 2)

    def halves(self, value, index):
        n = value.shape[0] // 2
        return lax.dynamic_slice_in_dim(value, index * n, n, 0)

    def sum_a(self, value):
        mine = self.halves(value, self.low) + self.pair(self.halves(value, 1 - self.low))
        mine = self.inward(mine)
        mine = mine + self.across(mine)
        mine = self.outward(mine)
        other = self.pair(mine)
        return mine, other, self.low

    def sum_b(self, value):
        value = self.inward(value)
        mine = self.halves(value, self.side) + self.across(self.halves(value, 1 - self.side))
        mine = mine + self.mid_pair(mine)
        other = self.across(mine)
        whole = jnp.where(
            self.side == 0,
            jnp.concatenate([mine, other], axis=0),
            jnp.concatenate([other, mine], axis=0),
        )
        return self.outward(whole)


def put(target, value, row, col):
    return lax.dynamic_update_slice(target, value.astype(target.dtype), (row, col))


def reduce_into(ring, target, value, row, col, kind):
    n = value.shape[0] // 2
    if kind == "a":
        mine, other, low = ring.sum_a(value)
        target = put(target, mine, row + low * n, col)
        return put(target, other, row + (1 - low) * n, col)
    return put(target, ring.sum_b(value), row, col)


def columns_of(ring, weight):
    rows, width = weight.shape
    part = width // ring.shards
    half = rows // 2

    def cols(k):
        return lax.dynamic_slice_in_dim(weight, (ring.shard ^ k) * part, part, 1)

    whole = jnp.zeros((ring.shards * rows, part), weight.dtype)
    far = {}
    for k in range(2, ring.shards):
        piece = ring.halves(cols(k), ring.low)
        got = ring.swap(piece, k)
        far[k] = (got, ring.pair(got))
    whole = put(whole, cols(0), ring.shard * rows, 0)
    whole = put(whole, ring.swap(cols(1), 1), (ring.shard ^ 1) * rows, 0)
    for k, (got, other) in far.items():
        base = (ring.shard ^ k) * rows
        whole = put(whole, got, base + ring.low * half, 0)
        whole = put(whole, other, base + (1 - ring.low) * half, 0)
    return whole


def gather_vector(ring, own):
    blocks = ring.gather(own[None])
    whole = jnp.zeros((ring.shards, own.shape[0]), own.dtype)
    for k, block in enumerate(blocks):
        whole = put(whole, block, ring.shard ^ k, 0)
    return whole.reshape(-1).astype(WIDE)


def shards(
    mesh,
    hidden_in,
    segments,
    cotangent,
    attn_gain,
    w_query,
    w_key,
    w_value,
    w_out,
    mlp_gain,
    w_gate,
    w_up,
    w_down,
):
    ring = Ring(mesh)
    count = ring.shards
    own_low = hidden_in[0]
    length, width = own_low.shape
    group = HEADS // KV_HEADS
    block = group * HEAD_DIM
    tokens = count * length
    factor = 1.0 / math.sqrt(HEAD_DIM)

    hidden_blocks = ring.gather(own_low)
    segment_ids = jnp.concatenate(ring.gather(segments), axis=0)
    gain1 = gather_vector(ring, attn_gain)
    gain2 = gather_vector(ring, mlp_gain)
    wq = columns_of(ring, w_query)
    wkv = jnp.concatenate([columns_of(ring, w_key), columns_of(ring, w_value)], axis=1)
    w_gate_cols = columns_of(ring, w_gate)
    w_up_cols = columns_of(ring, w_up)
    upstream_all = jnp.concatenate(ring.gather(cotangent[0]), axis=0)

    cosine, sine = angles(segment_ids)
    order = jnp.arange(length, dtype=jnp.int32)
    allowed = (
        (segment_ids[:, :, None] == segment_ids[:, None, :]) & (order[:, None] >= order[None, :])
    )[:, None]

    hidden_all = jnp.concatenate(hidden_blocks, axis=0).astype(WIDE)
    scale1_all = lax.rsqrt(jnp.mean(hidden_all * hidden_all, axis=1, keepdims=True) + EPS)
    normed1 = (hidden_all * scale1_all * gain1[None, :]).astype(LOW)

    query_raw = mm(normed1, wq)
    kv_raw = mm(normed1, wkv)
    cos_q, sin_q = cosine[:, :, None, :], sine[:, :, None, :]
    query = rotate(query_raw.reshape(count, length, group, HEAD_DIM), cos_q, sin_q).astype(LOW)
    keys = rotate(kv_raw[:, :HEAD_DIM].reshape(count, length, HEAD_DIM), cosine, sine).astype(LOW)
    values = kv_raw[:, HEAD_DIM:].reshape(count, length, HEAD_DIM).astype(LOW)

    raw = jnp.einsum("bqgd,bkd->bgqk", query, keys, preferred_element_type=WIDE) * factor
    masked = jnp.where(allowed, raw, -1000000000.0)
    peak = jnp.max(masked, axis=-1, keepdims=True)
    expo = jnp.exp(masked - peak)
    total = jnp.sum(expo, axis=-1, keepdims=True)
    probs = expo / total
    probs_low = probs.astype(LOW)
    log_total = peak + jnp.log(total)
    attended = (
        jnp.einsum("bgqk,bkd->bqgd", probs_low, values, preferred_element_type=WIDE)
        .reshape(tokens, block)
        .astype(LOW)
    )
    out_part = mm(attended, w_out).astype(LOW).reshape(count, length, width)
    near, far = ring.scatter([out_part[k] for k in range(count)])
    hidden = own_low.astype(WIDE)
    middle = hidden + (near.astype(WIDE) + far.astype(WIDE))
    scale2 = lax.rsqrt(jnp.mean(middle * middle, axis=1, keepdims=True) + EPS)
    unit2 = middle * scale2
    normed2 = jnp.concatenate(ring.gather((unit2 * gain2[None, :]).astype(LOW)), axis=0)

    gate = mm(normed2, w_gate_cols)
    upward = mm(normed2, w_up_cols)
    sigmoid_gate = jax.nn.sigmoid(gate)
    silu_gate = gate * sigmoid_gate
    inner = (silu_gate * upward).astype(LOW)
    grad_down = contract_rows(inner, upstream_all).astype(LOW)
    inner_grad = contract_cols(upstream_all, w_down)
    gate_grad = (inner_grad * upward * sigmoid_gate * (1.0 + gate * (1.0 - sigmoid_gate))).astype(
        LOW
    )
    up_grad = (inner_grad * silu_gate).astype(LOW)

    ff_own = w_down.shape[0]
    out_down = jnp.zeros(w_down.shape, WIDE)
    quarter = ff_own // 4
    for i in range(4):
        out_down = reduce_into(
            ring, out_down, grad_down[i * quarter : (i + 1) * quarter], i * quarter, 0, "ab"[i % 2]
        )

    back_part = (contract_cols(gate_grad, w_gate_cols) + contract_cols(up_grad, w_up_cols)).astype(
        LOW
    ).reshape(count, length, width)
    near, far = ring.scatter([back_part[k] for k in range(count)])
    normed2_grad = near.astype(WIDE) + far.astype(WIDE)

    rows = width // count

    def spread(normed, grad, out, kinds):
        cols = grad.shape[1]
        for k in (2, 3, 0, 1):
            where = ring.shard ^ k
            piece = lax.dynamic_slice_in_dim(normed, where * rows, rows, 1)
            slab = contract_rows(piece, grad).astype(LOW)
            if k:
                slab = ring.swap(slab, k)
            out = reduce_into(ring, out, slab, 0, where * cols, kinds[k])
        return out

    out_gate = spread(normed2, gate_grad, jnp.zeros(w_gate.shape, WIDE), "abab")
    out_up = spread(normed2, up_grad, jnp.zeros(w_up.shape, WIDE), "abab")

    down_part = mm(inner, w_down).astype(LOW).reshape(count, length, width)
    near, far = ring.scatter([down_part[k] for k in range(count)])
    layer_out = (middle + (near.astype(WIDE) + far.astype(WIDE))).astype(LOW)

    grad_mlp_gain = jnp.sum(normed2_grad * unit2, axis=0)
    middle_grad = cotangent[0].astype(WIDE) + norm_back(normed2_grad, gain2, unit2, scale2)
    branch_grad = jnp.concatenate(ring.gather(middle_grad.astype(LOW)), axis=0)
    grad_out = contract_rows(attended, branch_grad).astype(LOW)
    out_out = jnp.zeros(w_out.shape, WIDE)
    half = grad_out.shape[0] // 2
    for i in range(2):
        out_out = reduce_into(
            ring, out_out, grad_out[i * half : (i + 1) * half], i * half, 0, "ab"[i % 2]
        )
    attended_grad = (
        contract_cols(branch_grad, w_out).astype(LOW).reshape(count, length, group, HEAD_DIM)
    )
    probs = jnp.exp(masked - log_total)
    probs_grad = jnp.einsum("bqgd,bkd->bgqk", attended_grad, values, preferred_element_type=WIDE)
    inner_sum = jnp.sum(probs * probs_grad, axis=-1, keepdims=True)
    score_grad = (probs * (probs_grad - inner_sum)).astype(LOW)
    query_part = (
        jnp.einsum("bgqk,bkd->bqgd", score_grad, keys, preferred_element_type=WIDE) * factor
    )
    key_part = jnp.einsum("bgqk,bqgd->bkd", score_grad, query, preferred_element_type=WIDE) * factor
    value_part = jnp.einsum(
        "bgqk,bqgd->bkd", probs.astype(LOW), attended_grad, preferred_element_type=WIDE
    )
    query_grad = rotate(query_part, cos_q, -sin_q).astype(LOW).reshape(tokens, block)
    key_grad = rotate(key_part, cosine, -sine).astype(LOW).reshape(tokens, HEAD_DIM)
    value_grad = value_part.astype(LOW).reshape(tokens, HEAD_DIM)
    kv_grad = jnp.concatenate([key_grad, value_grad], axis=1)
    back_part = (contract_cols(query_grad, wq) + contract_cols(kv_grad, wkv)).astype(LOW).reshape(
        count, length, width
    )
    near, far = ring.scatter([back_part[k] for k in range(count)])
    normed1_grad = near.astype(WIDE) + far.astype(WIDE)

    out_query = spread(normed1, query_grad, jnp.zeros(w_query.shape, WIDE), "abab")
    kv_slabs = []
    for k in (2, 3, 0, 1):
        where = ring.shard ^ k
        piece = lax.dynamic_slice_in_dim(normed1, where * rows, rows, 1)
        slab = contract_rows(piece, kv_grad).astype(LOW)
        kv_slabs.append(ring.swap(slab, k) if k else slab)
    kv_sum = ring.sum_b(jnp.concatenate(kv_slabs, axis=1))
    out_key = jnp.zeros(w_key.shape, WIDE)
    out_value = jnp.zeros(w_value.shape, WIDE)
    for i, k in enumerate((2, 3, 0, 1)):
        col = (ring.shard ^ k) * HEAD_DIM
        base = i * 2 * HEAD_DIM
        out_key = put(out_key, kv_sum[:, base : base + HEAD_DIM], 0, col)
        out_value = put(out_value, kv_sum[:, base + HEAD_DIM : base + 2 * HEAD_DIM], 0, col)

    scale1 = lax.rsqrt(jnp.mean(hidden * hidden, axis=1, keepdims=True) + EPS)
    unit1 = hidden * scale1
    grad_attn_gain = jnp.sum(normed1_grad * unit1, axis=0)
    input_grad = middle_grad + norm_back(normed1_grad, gain1, unit1, scale1)

    gains = jnp.stack([grad_attn_gain, grad_mlp_gain]).reshape(2, count, rows)
    mine = gains[:, 0] * 0.0
    for k in range(count):
        part = lax.dynamic_index_in_dim(gains, ring.shard ^ k, 1, keepdims=False)
        mine = mine + (ring.swap(part, k) if k else part)
    mine = mine + ring.pair(mine)
    mine = ring.inward(mine)
    mine = mine + ring.across(mine)
    mine = ring.outward(mine)
    return (
        layer_out[None],
        input_grad[None],
        mine[0],
        out_query,
        out_key,
        out_value,
        out_out,
        mine[1],
        out_gate,
        out_up,
        out_down,
    )


def solution(mesh):
    both = ("shard", "rep")
    row, vec = P("shard", None), P("shard")
    act = P(both, None, None)
    in_specs = (act, P(both, None), act, vec, row, row, row, row, vec, row, row, row)
    out_specs = (act, act, vec, row, row, row, row, vec, row, row, row)

    def body(*args):
        return shards(mesh, *args)

    return jax.shard_map(
        body, mesh=mesh, in_specs=in_specs, out_specs=out_specs, check_vma=False
    )
```

```python
import math

import jax
import jax.numpy as jnp
from jax import lax
from jax.experimental import pallas as pl
from jax.sharding import PartitionSpec as P

HEADS = 32
KV_HEADS = 4
HEAD_DIM = 64
EPS = 1e-05
LOW = jnp.bfloat16
WIDE = jnp.float32


def mm(left, right):
    return jnp.dot(left, right, preferred_element_type=WIDE)


def contract_rows(left, right):
    return lax.dot_general(
        left, right, (((0,), (0,)), ((), ())), preferred_element_type=WIDE
    )


def contract_cols(left, right):
    return lax.dot_general(
        left, right, (((1,), (1,)), ((), ())), preferred_element_type=WIDE
    )


def angles(segment_ids):
    length = segment_ids.shape[-1]
    before = jnp.sum(
        (segment_ids[:, None, :] < segment_ids[:, :, None]).astype(jnp.int32), axis=2
    )
    place = (jnp.arange(length, dtype=jnp.int32)[None] - before).astype(WIDE)
    half = HEAD_DIM // 2
    freqs = 10000.0 ** (-jnp.arange(half, dtype=WIDE) / half)
    turn = place[..., None] * freqs
    return (jnp.cos(turn), jnp.sin(turn))


def rotate(values, cosine, sine):
    half = values.shape[-1] // 2
    first = values[..., :half]
    second = values[..., half:]
    return jnp.concatenate(
        [first * cosine - second * sine, second * cosine + first * sine], axis=-1
    )


def norm_back(normed_grad, gain, unit, scale):
    scaled = normed_grad * gain[None, :]
    return scale * (scaled - unit * jnp.mean(scaled * unit, axis=1, keepdims=True))


PUMPS = (1, 3, 4, 4, 1, 2, 2, 2, 4, 1, 1, 4)


def tie(*values):
    return lax.optimization_barrier(values)


def late(values, *marks):
    return list(tie(*values, *marks))[: len(values)]


def blank(shape):
    return pl.pallas_call(
        lambda out: None,
        out_shape=jax.ShapeDtypeStruct(shape, WIDE),
        out_specs=pl.BlockSpec(memory_space=pl.ANY),
        name="blank",
    )()


def put(target, value, row, col):
    return lax.dynamic_update_slice(target, value.astype(target.dtype), (row, col))


class Flow:
    def __init__(self):
        self.tasks = []
        self.turn = 0

    def add(self, task):
        self.tasks.append((task, next(task)))

    def advance(self, index, held):
        task, _ = self.tasks[index]
        try:
            self.tasks[index] = (task, task.send(held))
            self.turn = index + 1
        except StopIteration:
            del self.tasks[index]
            self.turn = index

    def pump(self, times, *values):
        for _ in range(times):
            if not self.tasks:
                break
            index = self.turn % len(self.tasks)
            held = self.tasks[index][1]
            tied = tie(*values, *held)
            values = tied[: len(values)]
            self.advance(index, tied[len(values) :])
        return values if len(values) != 1 else values[0]

    def after(self, *marks):
        self.tasks = [(task, late(held, *marks)) for task, held in self.tasks]

    def finish(self):
        while self.tasks:
            index = self.turn % len(self.tasks)
            self.advance(index, self.tasks[index][1])


class Ring:
    def __init__(self, mesh):
        self.shards = mesh.shape["shard"]
        self.reps = mesh.shape["rep"]
        self.line = self.reps // 2
        self.shard = lax.axis_index("shard")
        self.rep = lax.axis_index("rep")
        self.low = self.rep % 2
        self.high = self.rep // 2
        n = self.reps
        order = list(range(0, n, 2)) + list(range(n - 1, 0, -2))
        self.ways = [
            [(order[i], order[(i + step) % n]) for i in range(n)] for step in (1, -1)
        ]
        self.place = jnp.where(self.low == 0, self.high, n - 1 - self.high)

    def swap(self, value, k):
        return lax.ppermute(value, "shard", [(s, s ^ k) for s in range(self.shards)])

    def pair(self, value, k=1):
        return lax.ppermute(value, "rep", [(r, r ^ k) for r in range(self.reps)])

    def step(self, value, way):
        return lax.ppermute(value, "rep", self.ways[way])

    def gather(self, own):
        far = self.swap(own, 2)
        return [own, self.swap(own, 1), far, self.swap(far, 1)]

    def scatter(self, blocks, between=lambda v: v, flow=None):
        near = self.swap(jnp.concatenate([blocks[1], blocks[3]], axis=0), 1)
        n = blocks[0].shape[0]
        far = blocks[2] + near[n:]
        if flow is not None:
            flow.after(far)
        far = between(self.swap(far, 2))
        return blocks[0].astype(WIDE) + near[:n].astype(WIDE) + far.astype(WIDE)

    def ring_sum(self, value, between, store):
        n = self.reps
        signs = (-1, 1)

        def own(way, index):
            at = way * n + lax.rem(index + 4 * n, n)
            return lax.dynamic_index_in_dim(value, at, 1, keepdims=False)

        parts = [own(way, self.place + signs[way]) for way in (0, 1)]
        for s in range(n - 1):
            got = yield [self.step(parts[way], way) for way in (0, 1)]
            parts = [got[way] + own(way, self.place + signs[way] * (s + 2)) for way in (0, 1)]
        now = yield from between(parts)
        for way in (0, 1):
            store(way, self.place, now[way])
        for s in range(n - 1):
            now = yield [self.step(now[way], way) for way in (0, 1)]
            for way in (0, 1):
                at = lax.rem(self.place + signs[way] * (s + 1) + 4 * n, n)
                store(way, at, now[way])

    def exchange(self, parts, splits):
        count, rows, cols = parts[0].shape
        blocks = [
            [
                lax.dynamic_index_in_dim(part, self.shard ^ k, 0, keepdims=False)
                for part in parts
            ]
            for k in range(count)
        ]
        moved = [self.swap(jnp.stack(blocks[k]), k) for k in range(1, count)]
        moved = yield moved
        blocks[1:] = moved
        wholes = []
        for i in range(len(parts)):
            whole = jnp.zeros((rows, count * cols), parts[i].dtype)
            for k in range(count):
                for a, b in zip(splits, splits[1:]):
                    at = count * a + (self.shard ^ k) * (b - a)
                    whole = put(whole, blocks[k][i][:, a:b], 0, at)
            wholes.append(whole)
        return wholes


class Columns:
    def __init__(self, ring, weight, levels, after):
        self.ring = ring
        self.weight = weight
        self.rows = weight.shape[0]
        self.levels = levels
        self.size = self.rows >> levels
        share = sum(((ring.rep >> i) % 2) << i for i in range(levels))
        pieces = [self.cols(k, share * self.size, self.size) for k in range(2, ring.shards)]
        pieces = list(tie(*pieces, *after))[: len(pieces)]
        self.got = [[ring.swap(piece, k)] for k, piece in enumerate(pieces, 2)]
        self.near = ring.swap(tie(self.cols(1, 0, self.rows), *after)[0], 1)
        self.held = [share]

    def cols(self, k, start, size):
        part = self.weight.shape[1] // self.ring.shards
        return lax.dynamic_slice(self.weight, (start, (self.ring.shard ^ k) * part), (size, part))

    def settle(self, *values):
        flat = [piece for pieces in self.got for piece in pieces]
        tied = tie(*values, *flat)
        flat = list(tied[len(values) :])
        n = len(self.held)
        self.got = [flat[i * n : (i + 1) * n] for i in range(len(self.got))]
        return tied[: len(values)] if len(values) != 1 else tied[0]

    def after(self, *marks):
        self.near, *_ = late([self.near], *marks)
        self.got = [late(pieces, *marks) for pieces in self.got]
        self.weight, *_ = late([self.weight], *marks)

    def trade(self, level):
        bit = 1 << level
        self.got = [
            pieces + [self.ring.pair(piece, bit) for piece in pieces] for pieces in self.got
        ]
        self.held = self.held + [at ^ bit for at in self.held]

    def whole(self):
        ring = self.ring
        whole = jnp.zeros((ring.shards * self.rows, self.near.shape[1]), self.near.dtype)
        whole = put(whole, self.cols(0, 0, self.rows), ring.shard * self.rows, 0)
        whole = put(whole, self.near, (ring.shard ^ 1) * self.rows, 0)
        for k, pieces in enumerate(self.got, 2):
            for at, piece in zip(self.held, pieces):
                whole = put(whole, piece, (ring.shard ^ k) * self.rows + at * self.size, 0)
        return whole


def shards(
    mesh,
    hidden_in,
    segments,
    cotangent,
    attn_gain,
    w_query,
    w_key,
    w_value,
    w_out,
    mlp_gain,
    w_gate,
    w_up,
    w_down,
):
    ring = Ring(mesh)
    flow = Flow()
    count = ring.shards
    reps = ring.reps
    own_low = hidden_in[0]
    length, width = own_low.shape
    group = HEADS // KV_HEADS
    block = group * HEAD_DIM
    tokens = count * length
    rows = width // count
    factor = 1.0 / math.sqrt(HEAD_DIM)

    hidden_blocks = ring.gather(own_low)
    segment_ids = jnp.concatenate(ring.gather(segments), axis=0)
    gains = jnp.stack([attn_gain, mlp_gain])
    gain_blocks = ring.gather(gains)
    whole_gain = jnp.zeros((2, width), gains.dtype)
    for k, piece in enumerate(gain_blocks):
        whole_gain = put(whole_gain, piece, 0, (ring.shard ^ k) * rows)
    gain1 = whole_gain[0].astype(WIDE)
    gain2 = whole_gain[1].astype(WIDE)
    w_qkv = jnp.concatenate(
        [
            w_query.reshape(rows, count, block),
            w_key.reshape(rows, count, HEAD_DIM),
            w_value.reshape(rows, count, HEAD_DIM),
        ],
        axis=2,
    ).reshape(rows, count * (block + 2 * HEAD_DIM))
    w_qkv_cols = Columns(ring, w_qkv, 0, []).whole()

    cosine, sine = angles(segment_ids)
    order = jnp.arange(length, dtype=jnp.int32)
    allowed = (
        (segment_ids[:, :, None] == segment_ids[:, None, :]) & (order[:, None] >= order[None, :])
    )[:, None]

    hidden_all = jnp.concatenate(hidden_blocks, axis=0).astype(WIDE)
    scale1_all = lax.rsqrt(jnp.mean(hidden_all * hidden_all, axis=1, keepdims=True) + EPS)
    normed1 = (hidden_all * scale1_all * gain1[None, :]).astype(LOW)

    gate_cols = Columns(ring, w_gate, 2, [hidden_blocks[2]])
    up_cols = Columns(ring, w_up, 2, [hidden_blocks[2]])

    qkv_raw = mm(normed1, w_qkv_cols)
    query_raw, kv_raw = qkv_raw[:, :block], qkv_raw[:, block:]
    cos_q, sin_q = cosine[:, :, None, :], sine[:, :, None, :]
    query = rotate(query_raw.reshape(count, length, group, HEAD_DIM), cos_q, sin_q).astype(LOW)
    keys = rotate(kv_raw[:, :HEAD_DIM].reshape(count, length, HEAD_DIM), cosine, sine).astype(LOW)
    values = kv_raw[:, HEAD_DIM:].reshape(count, length, HEAD_DIM).astype(LOW)
    query = gate_cols.settle(query)
    gate_cols.trade(0)

    raw = jnp.einsum("bqgd,bkd->bgqk", query, keys, preferred_element_type=WIDE) * factor
    masked = jnp.where(allowed, raw, -1000000000.0)
    peak = jnp.max(masked, axis=-1, keepdims=True)
    expo = jnp.exp(masked - peak)
    total = jnp.sum(expo, axis=-1, keepdims=True)
    probs = expo / total
    probs_low = up_cols.settle(probs.astype(LOW))
    up_cols.trade(0)
    log_total = peak + jnp.log(total)
    attended = (
        jnp.einsum("bgqk,bkd->bqgd", probs_low, values, preferred_element_type=WIDE)
        .reshape(tokens, block)
        .astype(LOW)
    )
    attended = gate_cols.settle(attended)
    gate_cols.trade(1)
    out_part = mm(attended, w_out).astype(LOW).reshape(count, length, width)
    reduced = ring.scatter([out_part[k] for k in range(count)], up_cols.settle)
    up_cols.trade(1)
    outs = {
        "query": blank(w_query.shape),
        "key": blank(w_key.shape),
        "value": blank(w_value.shape),
        "out": blank((rows, width)),
        "gate": blank(w_gate.shape),
        "up": blank(w_up.shape),
        "down": blank(w_down.shape),
    }
    hidden = own_low.astype(WIDE)
    middle = hidden + reduced
    scale2 = lax.rsqrt(jnp.mean(middle * middle, axis=1, keepdims=True) + EPS)
    unit2 = middle * scale2
    normed2_own = (unit2 * gain2[None, :]).astype(LOW)
    normed2_blocks = ring.gather(normed2_own)
    upstream_own, _ = tie(cotangent[0], normed2_blocks[2])
    upstream_blocks = ring.gather(upstream_own)
    normed2 = jnp.concatenate(normed2_blocks, axis=0)

    ff_own = w_down.shape[0]
    gate_cols.after(normed2_own)
    up_cols.after(normed2_own)
    w_gate_cols = gate_cols.whole()
    w_up_cols = up_cols.whole()
    gate = mm(normed2, w_gate_cols)
    upstream_all = jnp.concatenate(late(upstream_blocks, gate), axis=0)
    upward = mm(normed2, w_up_cols)
    sigmoid_gate = jax.nn.sigmoid(gate)
    silu_gate = gate * sigmoid_gate
    inner = (silu_gate * upward).astype(LOW)

    def unpack(names, widths, n):
        def store(way, index, value):
            at = 0
            for name, cols in zip(names, widths):
                piece = value[:, at : at + cols]
                outs[name] = put(outs[name], piece, (way * reps + index) * n, 0)
                at += cols

        return store

    def first_blocks(parts):
        yield from ()
        return [part[0] for part in parts]

    grad_down = contract_rows(inner, upstream_all).astype(LOW)
    n_down = ff_own // (2 * reps)
    flow.add(
        ring.ring_sum(
            grad_down.reshape(1, 2 * reps, n_down, width),
            first_blocks,
            unpack(["down"], [width], n_down),
        )
    )
    upstream_next, grad_down = tie(upstream_all, grad_down)
    inner_grad = contract_cols(upstream_next, w_down)
    gate_grad = (inner_grad * upward * sigmoid_gate * (1.0 + gate * (1.0 - sigmoid_gate))).astype(
        LOW
    )
    up_grad = (inner_grad * silu_gate).astype(LOW)
    gate_grad, up_grad = flow.pump(2, gate_grad, up_grad)

    n_rows = rows // (2 * reps)
    for name, cols in (("gate", gate_grad), ("up", up_grad)):
        full = contract_rows(normed2, cols).astype(LOW)
        full, gate_grad, up_grad = tie(full, gate_grad, up_grad)
        flow.add(
            ring.ring_sum(
                full.reshape(count, 2 * reps, n_rows, ff_own),
                lambda v: ring.exchange(v, (0, ff_own)),
                unpack([name], [count * ff_own], n_rows),
            )
        )
        gate_grad, up_grad = flow.pump(PUMPS[0], gate_grad, up_grad)

    back_part = (contract_cols(gate_grad, w_gate_cols) + contract_cols(up_grad, w_up_cols)).astype(
        LOW
    )
    back_part = flow.pump(PUMPS[1], back_part).reshape(count, length, width)
    normed2_grad = ring.scatter([back_part[k] for k in range(count)], lambda v: flow.pump(PUMPS[2], v), flow)

    grad_mlp_gain = jnp.sum(normed2_grad * unit2, axis=0)
    middle_grad = cotangent[0].astype(WIDE) + norm_back(normed2_grad, gain2, unit2, scale2)
    middle_low = middle_grad.astype(LOW)
    flow.after(middle_low)
    branch_blocks = ring.gather(middle_low)
    branch_blocks = flow.pump(PUMPS[3], *branch_blocks)
    branch_grad = jnp.concatenate(branch_blocks, axis=0)
    attended_grad = (
        contract_cols(branch_grad, w_out).astype(LOW).reshape(count, length, group, HEAD_DIM)
    )
    attended_grad = flow.pump(PUMPS[4], attended_grad)
    probs = jnp.exp(masked - log_total)
    probs_grad = jnp.einsum("bqgd,bkd->bgqk", attended_grad, values, preferred_element_type=WIDE)
    inner_sum = jnp.sum(probs * probs_grad, axis=-1, keepdims=True)
    score_grad = (probs * (probs_grad - inner_sum)).astype(LOW)
    score_grad = flow.pump(PUMPS[5], score_grad)
    query_part = (
        jnp.einsum("bgqk,bkd->bqgd", score_grad, keys, preferred_element_type=WIDE) * factor
    )
    key_part = jnp.einsum("bgqk,bqgd->bkd", score_grad, query, preferred_element_type=WIDE) * factor
    value_part = jnp.einsum(
        "bgqk,bqgd->bkd", probs.astype(LOW), attended_grad, preferred_element_type=WIDE
    )
    query_grad = rotate(query_part, cos_q, -sin_q).astype(LOW).reshape(tokens, block)
    key_grad = rotate(key_part, cosine, -sine).astype(LOW).reshape(tokens, HEAD_DIM)
    value_grad = value_part.astype(LOW).reshape(tokens, HEAD_DIM)
    qkv_grad = jnp.concatenate([query_grad, key_grad, value_grad], axis=1)
    qkv_grad = flow.pump(PUMPS[6], qkv_grad)

    grad_qkv = contract_rows(normed1, qkv_grad).astype(LOW)
    grad_out = contract_rows(attended, branch_grad).astype(LOW)
    grad_qkv, grad_out, qkv_grad = flow.pump(PUMPS[7], grad_qkv, grad_out, qkv_grad)
    qkv_cols = qkv_grad.shape[1]
    attn_full = jnp.concatenate(
        [
            grad_qkv.reshape(count, 2 * reps, n_rows, qkv_cols),
            jnp.transpose(grad_out.reshape(2 * reps, n_rows, count, rows), (2, 0, 1, 3)),
        ],
        axis=3,
    )

    def attn_message(parts):
        moved = yield from ring.exchange(
            [part[:, :, :qkv_cols] for part in parts], (0, block, block + HEAD_DIM, qkv_cols)
        )
        still = [
            jnp.transpose(part[:, :, qkv_cols:], (1, 0, 2)).reshape(n_rows, width)
            for part in parts
        ]
        return [jnp.concatenate(both, axis=1) for both in zip(moved, still)]

    flow.add(
        ring.ring_sum(
            attn_full,
            attn_message,
            unpack(
                ["query", "key", "value", "out"],
                [w_query.shape[1], w_key.shape[1], w_value.shape[1], width],
                n_rows,
            ),
        )
    )

    back_part = contract_cols(qkv_grad, w_qkv_cols).astype(LOW)
    back_part = flow.pump(1, back_part).reshape(count, length, width)
    normed1_grad = ring.scatter([back_part[k] for k in range(count)], lambda v: flow.pump(PUMPS[8], v), flow)
    scale1 = lax.rsqrt(jnp.mean(hidden * hidden, axis=1, keepdims=True) + EPS)
    unit1 = hidden * scale1
    grad_attn_gain = jnp.sum(normed1_grad * unit1, axis=0)
    input_grad = middle_grad + norm_back(normed1_grad, gain1, unit1, scale1)
    input_grad, inner = flow.pump(PUMPS[9], input_grad, inner)

    down_part = mm(inner, w_down).astype(LOW)
    down_part = flow.pump(PUMPS[10], down_part).reshape(count, length, width)
    layer_out = (
        middle + ring.scatter([down_part[k] for k in range(count)], lambda v: flow.pump(PUMPS[11], v), flow)
    ).astype(LOW)

    both = jnp.stack([grad_attn_gain, grad_mlp_gain])
    k = 1
    while k < count:
        both = both + ring.swap(both, k)
        k *= 2
    mine = lax.dynamic_slice_in_dim(both, ring.shard * rows, rows, 1)
    k = 1
    while k < reps:
        mine = mine + ring.pair(mine, k)
        k *= 2
    flow.finish()

    return (
        layer_out[None],
        input_grad[None],
        mine[0],
        outs["query"],
        outs["key"],
        outs["value"],
        outs["out"],
        mine[1],
        outs["gate"],
        outs["up"],
        outs["down"],
    )


def solution(mesh):
    both = ("shard", "rep")
    row, vec = P("shard", None), P("shard")
    act = P(both, None, None)
    in_specs = (act, P(both, None), act, vec, row, row, row, row, vec, row, row, row)
    out_specs = (act, act, vec, row, row, row, row, vec, row, row, row)

    def body(*args):
        return shards(mesh, *args)

    return jax.shard_map(
        body, mesh=mesh, in_specs=in_specs, out_specs=out_specs, check_vma=False
    )
```

```python
import math

import jax
import jax.numpy as jnp
from jax import lax
from jax.experimental import pallas as pl
from jax.sharding import PartitionSpec as P

HEADS = 32
KV_HEADS = 4
HEAD_DIM = 64
EPS = 1e-05
LOW = jnp.bfloat16
WIDE = jnp.float32


def mm(left, right):
    return jnp.dot(left, right, preferred_element_type=WIDE)


def contract_rows(left, right):
    return lax.dot_general(
        left, right, (((0,), (0,)), ((), ())), preferred_element_type=WIDE
    )


def contract_cols(left, right):
    return lax.dot_general(
        left, right, (((1,), (1,)), ((), ())), preferred_element_type=WIDE
    )


def angles(segment_ids):
    length = segment_ids.shape[-1]
    before = jnp.sum(
        (segment_ids[:, None, :] < segment_ids[:, :, None]).astype(jnp.int32), axis=2
    )
    place = (jnp.arange(length, dtype=jnp.int32)[None] - before).astype(WIDE)
    half = HEAD_DIM // 2
    freqs = 10000.0 ** (-jnp.arange(half, dtype=WIDE) / half)
    turn = place[..., None] * freqs
    return (jnp.cos(turn), jnp.sin(turn))


def rotate(values, cosine, sine):
    half = values.shape[-1] // 2
    first = values[..., :half]
    second = values[..., half:]
    return jnp.concatenate(
        [first * cosine - second * sine, second * cosine + first * sine], axis=-1
    )


def norm_back(normed_grad, gain, unit, scale):
    scaled = normed_grad * gain[None, :]
    return scale * (scaled - unit * jnp.mean(scaled * unit, axis=1, keepdims=True))


PUMPS = (1, 2, 2, 2, 2, 2, 2, 1, 3, 0, 2, 3, 3, 1)


def tie(*values):
    return lax.optimization_barrier(values)


def late(values, *marks):
    return list(tie(*values, *marks))[: len(values)]


def blank(shape):
    return pl.pallas_call(
        lambda out: None,
        out_shape=jax.ShapeDtypeStruct(shape, WIDE),
        out_specs=pl.BlockSpec(memory_space=pl.ANY),
        name="blank",
    )()


def put(target, value, row, col):
    return lax.dynamic_update_slice(target, value.astype(target.dtype), (row, col))


class Flow:
    def __init__(self):
        self.tasks = []
        self.turn = 0

    def add(self, task):
        self.tasks.append((task, *next(task)))

    def advance(self, index, held):
        task = self.tasks[index][0]
        try:
            self.tasks[index] = (task, *task.send(held))
            self.turn = index + 1
            return self.tasks[index][2]
        except StopIteration:
            del self.tasks[index]
            self.turn = index
            return []

    def pump(self, times, *values):
        sent = []
        for _ in range(times):
            if not self.tasks:
                break
            index = self.turn % len(self.tasks)
            held = self.tasks[index][1]
            tied = tie(*values, *held)
            values = tied[: len(values)]
            sent += self.advance(index, tied[len(values) :])
        if sent:
            values = late(values, *sent)
        return values if len(values) != 1 else values[0]

    def after(self, *marks):
        self.tasks = [(task, late(held, *marks), sent) for task, held, sent in self.tasks]

    def finish(self):
        while self.tasks:
            index = self.turn % len(self.tasks)
            self.advance(index, self.tasks[index][1])


class Ring:
    def __init__(self, mesh):
        self.shards = mesh.shape["shard"]
        self.reps = mesh.shape["rep"]
        self.line = self.reps // 2
        self.shard = lax.axis_index("shard")
        self.rep = lax.axis_index("rep")
        self.low = self.rep % 2
        self.high = self.rep // 2
        n = self.reps
        order = list(range(0, n, 2)) + list(range(n - 1, 0, -2))
        self.ways = [
            [(order[i], order[(i + step) % n]) for i in range(n)] for step in (1, -1)
        ]
        self.place = jnp.where(self.low == 0, self.high, n - 1 - self.high)

    def swap(self, value, k):
        return lax.ppermute(value, "shard", [(s, s ^ k) for s in range(self.shards)])

    def pair(self, value, k=1):
        return lax.ppermute(value, "rep", [(r, r ^ k) for r in range(self.reps)])

    def step(self, value, way):
        return lax.ppermute(value, "rep", self.ways[way])

    def gather(self, own):
        far = self.swap(own, 2)
        return [own, self.swap(own, 1), far, self.swap(far, 1)]

    def scatter(self, blocks, between=lambda v: v, flow=None):
        near = self.swap(jnp.concatenate([blocks[1], blocks[3]], axis=0), 1)
        n = blocks[0].shape[0]
        far = blocks[2] + near[n:]
        if flow is not None:
            flow.after(far)
        far = between(self.swap(far, 2))
        return blocks[0].astype(WIDE) + near[:n].astype(WIDE) + far.astype(WIDE)

    def ring_sum(self, chunk, between, store):
        n = self.reps
        signs = (-1, 1)

        def own(way, index):
            return chunk(way * n + lax.rem(index + 4 * n, n))

        parts = [own(way, self.place + signs[way]) for way in (0, 1)]
        for s in range(n - 1):
            got = yield [self.step(parts[way], way) for way in (0, 1)], parts
            parts = [got[way] + own(way, self.place + signs[way] * (s + 2)) for way in (0, 1)]
        now = yield from between(parts)
        for way in (0, 1):
            store(way, self.place, now[way])
        for s in range(n - 1):
            now = yield [self.step(now[way], way) for way in (0, 1)], now
            for way in (0, 1):
                at = lax.rem(self.place + signs[way] * (s + 1) + 4 * n, n)
                store(way, at, now[way])

    def exchange(self, parts, splits):
        count, rows, cols = parts[0].shape
        blocks = [
            [
                lax.dynamic_index_in_dim(part, self.shard ^ k, 0, keepdims=False)
                for part in parts
            ]
            for k in range(count)
        ]
        sent = [jnp.stack(blocks[k]) for k in range(1, count)]
        moved = yield [self.swap(item, k) for k, item in enumerate(sent, 1)], sent
        blocks[1:] = moved
        wholes = []
        for i in range(len(parts)):
            whole = jnp.zeros((rows, count * cols), parts[i].dtype)
            for k in range(count):
                for a, b in zip(splits, splits[1:]):
                    at = count * a + (self.shard ^ k) * (b - a)
                    whole = put(whole, blocks[k][i][:, a:b], 0, at)
            wholes.append(whole)
        return wholes


class Columns:
    def __init__(self, ring, weight, bits):
        self.ring = ring
        self.weight = weight
        self.rows = weight.shape[0]
        self.bits = bits
        self.size = self.rows >> len(bits)
        share = sum(((ring.rep // bit) % 2) << i for i, bit in enumerate(bits))
        pieces = [self.cols(k, share * self.size, self.size) for k in range(2, ring.shards)]
        self.got = [[ring.swap(piece, k)] for k, piece in enumerate(pieces, 2)]
        self.near = ring.swap(self.cols(1, 0, self.rows), 1)
        self.held = [share]

    def cols(self, k, start, size):
        part = self.weight.shape[1] // self.ring.shards
        return lax.dynamic_slice(self.weight, (start, (self.ring.shard ^ k) * part), (size, part))

    def settle(self, *values, only=None):
        for i in range(len(self.got)) if only is None else [only]:
            tied = tie(*values, *self.got[i])
            values, self.got[i] = tied[: len(values)], list(tied[len(values) :])
        return values if len(values) != 1 else values[0]

    def after(self, *marks):
        self.near, *_ = late([self.near], *marks)
        self.got = [late(pieces, *marks) for pieces in self.got]
        self.weight, *_ = late([self.weight], *marks)

    def trade(self, level):
        bit = self.bits[level]
        self.got = [
            pieces + [self.ring.pair(piece, bit) for piece in pieces] for pieces in self.got
        ]
        self.held = self.held + [at ^ (1 << level) for at in self.held]

    def whole(self):
        ring = self.ring
        whole = jnp.zeros((ring.shards * self.rows, self.near.shape[1]), self.near.dtype)
        whole = put(whole, self.cols(0, 0, self.rows), ring.shard * self.rows, 0)
        whole = put(whole, self.near, (ring.shard ^ 1) * self.rows, 0)
        for k, pieces in enumerate(self.got, 2):
            for at, piece in zip(self.held, pieces):
                whole = put(whole, piece, (ring.shard ^ k) * self.rows + at * self.size, 0)
        return whole


def shards(
    mesh,
    hidden_in,
    segments,
    cotangent,
    attn_gain,
    w_query,
    w_key,
    w_value,
    w_out,
    mlp_gain,
    w_gate,
    w_up,
    w_down,
):
    ring = Ring(mesh)
    flow = Flow()
    count = ring.shards
    reps = ring.reps
    own_low = hidden_in[0]
    length, width = own_low.shape
    group = HEADS // KV_HEADS
    block = group * HEAD_DIM
    tokens = count * length
    rows = width // count
    factor = 1.0 / math.sqrt(HEAD_DIM)

    hidden_blocks = ring.gather(own_low)
    segment_ids = jnp.concatenate(ring.gather(segments), axis=0)
    gains = jnp.stack([attn_gain, mlp_gain])
    gain_blocks = ring.gather(gains)
    whole_gain = jnp.zeros((2, width), gains.dtype)
    for k, piece in enumerate(gain_blocks):
        whole_gain = put(whole_gain, piece, 0, (ring.shard ^ k) * rows)
    gain1 = whole_gain[0].astype(WIDE)
    gain2 = whole_gain[1].astype(WIDE)
    w_kv = jnp.concatenate(
        [
            w_key.reshape(rows, count, HEAD_DIM),
            w_value.reshape(rows, count, HEAD_DIM),
        ],
        axis=2,
    ).reshape(rows, count * 2 * HEAD_DIM)
    query_cols = Columns(ring, w_query, ())
    kv_cols = Columns(ring, w_kv, ())
    hidden_blocks = query_cols.settle(*hidden_blocks)
    hidden_blocks = kv_cols.settle(*hidden_blocks)
    gate_cols = Columns(ring, w_gate, (2,))
    up_cols = Columns(ring, w_up, (1,))
    w_query_cols = query_cols.whole()
    w_kv_cols = kv_cols.whole()

    cosine, sine = angles(segment_ids)
    order = jnp.arange(length, dtype=jnp.int32)
    allowed = (
        (segment_ids[:, :, None] == segment_ids[:, None, :]) & (order[:, None] >= order[None, :])
    )[:, None]

    hidden_all = jnp.concatenate(hidden_blocks, axis=0).astype(WIDE)
    scale1_all = lax.rsqrt(jnp.mean(hidden_all * hidden_all, axis=1, keepdims=True) + EPS)
    normed1 = (hidden_all * scale1_all * gain1[None, :]).astype(LOW)

    query_raw = mm(normed1, w_query_cols)
    kv_raw = mm(normed1, w_kv_cols)
    cos_q, sin_q = cosine[:, :, None, :], sine[:, :, None, :]
    query = rotate(query_raw.reshape(count, length, group, HEAD_DIM), cos_q, sin_q).astype(LOW)
    keys = rotate(kv_raw[:, :HEAD_DIM].reshape(count, length, HEAD_DIM), cosine, sine).astype(LOW)
    values = kv_raw[:, HEAD_DIM:].reshape(count, length, HEAD_DIM).astype(LOW)
    query = gate_cols.settle(query)
    gate_cols.trade(0)

    raw = jnp.einsum("bqgd,bkd->bgqk", query, keys, preferred_element_type=WIDE) * factor
    masked = jnp.where(allowed, raw, -1000000000.0)
    peak = jnp.max(masked, axis=-1, keepdims=True)
    expo = jnp.exp(masked - peak)
    total = jnp.sum(expo, axis=-1, keepdims=True)
    probs = expo / total
    probs_low = probs.astype(LOW)
    log_total = peak + jnp.log(total)
    attended = (
        jnp.einsum("bgqk,bkd->bqgd", probs_low, values, preferred_element_type=WIDE)
        .reshape(tokens, block)
        .astype(LOW)
    )
    attended = gate_cols.settle(attended, only=0)
    out_part = up_cols.settle(mm(attended, w_out).astype(LOW)).reshape(count, length, width)
    up_cols.trade(0)
    reduced = ring.scatter(
        [out_part[k] for k in range(count)], gate_cols.settle
    )
    outs = {
        "query": blank(w_query.shape),
        "key": blank(w_key.shape),
        "value": blank(w_value.shape),
        "out": blank((rows, width)),
        "gate": blank(w_gate.shape),
        "up": blank(w_up.shape),
        "down": blank(w_down.shape),
    }
    hidden = own_low.astype(WIDE)
    middle = hidden + reduced
    scale2 = lax.rsqrt(jnp.mean(middle * middle, axis=1, keepdims=True) + EPS)
    unit2 = middle * scale2
    normed2_own = (unit2 * gain2[None, :]).astype(LOW)
    normed2_blocks = ring.gather(normed2_own)
    (upstream_own,) = late([cotangent[0]], normed2_blocks[2])
    upstream_far = ring.swap(upstream_own, 2)
    normed2 = jnp.concatenate(normed2_blocks, axis=0)

    ff_own = w_down.shape[0]
    gate_cols.after(normed2_own)
    up_cols.after(normed2_own)
    w_gate_cols = gate_cols.whole()
    w_up_cols = up_cols.whole()
    gate = mm(normed2, w_gate_cols)
    upward = mm(normed2, w_up_cols)
    sigmoid_gate = jax.nn.sigmoid(gate)
    silu_gate = gate * sigmoid_gate
    inner = (silu_gate * upward).astype(LOW)
    (upstream_far,) = late([upstream_far], inner)
    upstream_all = jnp.concatenate(
        [
            upstream_own,
            ring.swap(upstream_own, 1),
            upstream_far,
            ring.swap(upstream_far, 1),
        ],
        axis=0,
    )

    def unpack(names, widths, n):
        def store(way, index, value):
            at = 0
            for name, cols in zip(names, widths):
                piece = value[:, at : at + cols]
                outs[name] = put(outs[name], piece, (way * reps + index) * n, 0)
                at += cols

        return store

    def first_blocks(parts):
        yield from ()
        return [part[0] for part in parts]

    grad_down = contract_rows(inner, upstream_all).astype(LOW)
    def chunk_of(value, axis):
        n = value.shape[axis] // (2 * reps)
        return lambda index: lax.dynamic_slice_in_dim(value, index * n, n, axis)

    n_down = ff_own // (2 * reps)
    flow.add(
        ring.ring_sum(
            chunk_of(grad_down[None], 1), first_blocks, unpack(["down"], [width], n_down)
        )
    )
    upstream_next, grad_down = tie(upstream_all, grad_down)
    inner_grad = contract_cols(upstream_next, w_down)
    gate_grad = (inner_grad * upward * sigmoid_gate * (1.0 + gate * (1.0 - sigmoid_gate))).astype(
        LOW
    )
    up_grad = (inner_grad * silu_gate).astype(LOW)
    gate_grad, up_grad = flow.pump(2, gate_grad, up_grad)

    n_rows = rows // (2 * reps)
    fulls = []
    for cols in (gate_grad, up_grad):
        full = contract_rows(normed2, cols).astype(LOW).reshape(count, rows, ff_own)
        full, gate_grad, up_grad = flow.pump(PUMPS[0], full, gate_grad, up_grad)
        fulls.append(chunk_of(full, 1))
    flow.add(
        ring.ring_sum(
            lambda index: jnp.concatenate([full(index) for full in fulls], axis=2),
            lambda v: ring.exchange(v, (0, ff_own, 2 * ff_own)),
            unpack(["gate", "up"], [count * ff_own] * 2, n_rows),
        )
    )

    back_part = contract_cols(gate_grad, w_gate_cols)
    back_part, up_grad = flow.pump(PUMPS[13], back_part, up_grad)
    back_part = (back_part + contract_cols(up_grad, w_up_cols)).astype(LOW)
    back_part = flow.pump(PUMPS[1], back_part).reshape(count, length, width)
    normed2_grad = ring.scatter([back_part[k] for k in range(count)], lambda v: flow.pump(PUMPS[2], v), flow)

    grad_mlp_gain = jnp.sum(normed2_grad * unit2, axis=0)
    middle_grad = cotangent[0].astype(WIDE) + norm_back(normed2_grad, gain2, unit2, scale2)
    middle_low = middle_grad.astype(LOW)
    flow.after(middle_low)
    branch_far = flow.pump(PUMPS[3], ring.swap(middle_low, 2))
    branch_grad = jnp.concatenate(
        [middle_low, ring.swap(middle_low, 1), branch_far, ring.swap(branch_far, 1)], axis=0
    )
    attended_grad = (
        contract_cols(branch_grad, w_out).astype(LOW).reshape(count, length, group, HEAD_DIM)
    )
    attended_grad = flow.pump(PUMPS[4], attended_grad)
    probs = jnp.exp(masked - log_total)
    probs_grad = jnp.einsum("bqgd,bkd->bgqk", attended_grad, values, preferred_element_type=WIDE)
    inner_sum = jnp.sum(probs * probs_grad, axis=-1, keepdims=True)
    score_grad = (probs * (probs_grad - inner_sum)).astype(LOW)
    score_grad = flow.pump(PUMPS[5], score_grad)
    query_part = (
        jnp.einsum("bgqk,bkd->bqgd", score_grad, keys, preferred_element_type=WIDE) * factor
    )
    key_part = jnp.einsum("bgqk,bqgd->bkd", score_grad, query, preferred_element_type=WIDE) * factor
    value_part = jnp.einsum(
        "bgqk,bqgd->bkd", probs.astype(LOW), attended_grad, preferred_element_type=WIDE
    )
    query_grad = rotate(query_part, cos_q, -sin_q).astype(LOW).reshape(tokens, block)
    key_grad = rotate(key_part, cosine, -sine).astype(LOW).reshape(tokens, HEAD_DIM)
    value_grad = value_part.astype(LOW).reshape(tokens, HEAD_DIM)
    qkv_grad = jnp.concatenate([query_grad, key_grad, value_grad], axis=1)
    qkv_grad = flow.pump(PUMPS[6], qkv_grad)

    grad_qkv = contract_rows(normed1, qkv_grad).astype(LOW)
    grad_out = contract_rows(attended, branch_grad).astype(LOW)
    grad_qkv, grad_out, qkv_grad = flow.pump(PUMPS[7], grad_qkv, grad_out, qkv_grad)
    qkv_cols = qkv_grad.shape[1]
    qkv_chunk = chunk_of(grad_qkv.reshape(count, rows, qkv_cols), 1)
    out_chunk = chunk_of(grad_out, 0)

    def attn_chunk(index):
        out = jnp.transpose(out_chunk(index).reshape(n_rows, count, rows), (1, 0, 2))
        return jnp.concatenate([qkv_chunk(index), out], axis=2)

    def attn_message(parts):
        moved = yield from ring.exchange(
            [part[:, :, :qkv_cols] for part in parts], (0, block, block + HEAD_DIM, qkv_cols)
        )
        still = [
            jnp.transpose(part[:, :, qkv_cols:], (1, 0, 2)).reshape(n_rows, width)
            for part in parts
        ]
        return [jnp.concatenate(both, axis=1) for both in zip(moved, still)]

    flow.add(
        ring.ring_sum(
            attn_chunk,
            attn_message,
            unpack(
                ["query", "key", "value", "out"],
                [w_query.shape[1], w_key.shape[1], w_value.shape[1], width],
                n_rows,
            ),
        )
    )

    qkv_grad = flow.pump(PUMPS[12], qkv_grad)
    back_part = (
        contract_cols(qkv_grad[:, :block], w_query_cols)
        + contract_cols(qkv_grad[:, block:], w_kv_cols)
    ).astype(LOW)
    back_part = flow.pump(1, back_part).reshape(count, length, width)
    normed1_grad = ring.scatter([back_part[k] for k in range(count)], lambda v: flow.pump(PUMPS[8], v), flow)
    scale1 = lax.rsqrt(jnp.mean(hidden * hidden, axis=1, keepdims=True) + EPS)
    unit1 = hidden * scale1
    grad_attn_gain = jnp.sum(normed1_grad * unit1, axis=0)
    input_grad = middle_grad + norm_back(normed1_grad, gain1, unit1, scale1)
    (inner,) = late([inner], input_grad)

    down_part = mm(inner, w_down).astype(LOW)
    down_part = flow.pump(PUMPS[10], down_part).reshape(count, length, width)
    layer_out = (
        middle + ring.scatter([down_part[k] for k in range(count)], lambda v: flow.pump(PUMPS[11], v), flow)
    ).astype(LOW)

    both = jnp.stack([grad_attn_gain, grad_mlp_gain])
    k = 1
    while k < count:
        both = both + ring.swap(both, k)
        k *= 2
    mine = lax.dynamic_slice_in_dim(both, ring.shard * rows, rows, 1)
    k = 1
    while k < reps:
        mine = mine + ring.pair(mine, k)
        k *= 2
    flow.finish()

    return (
        layer_out[None],
        input_grad[None],
        mine[0],
        outs["query"],
        outs["key"],
        outs["value"],
        outs["out"],
        mine[1],
        outs["gate"],
        outs["up"],
        outs["down"],
    )


def solution(mesh):
    both = ("shard", "rep")
    row, vec = P("shard", None), P("shard")
    act = P(both, None, None)
    in_specs = (act, P(both, None), act, vec, row, row, row, row, vec, row, row, row)
    out_specs = (act, act, vec, row, row, row, row, vec, row, row, row)

    def body(*args):
        return shards(mesh, *args)

    return jax.shard_map(
        body, mesh=mesh, in_specs=in_specs, out_specs=out_specs, check_vma=False
    )
```

```python
import math

import jax
import jax.numpy as jnp
from jax import lax
from jax.experimental import pallas as pl
from jax.sharding import PartitionSpec as P

HEADS = 32
KV_HEADS = 4
HEAD_DIM = 64
EPS = 1e-05
LOW = jnp.bfloat16
WIDE = jnp.float32


def mm(left, right):
    return jnp.dot(left, right, preferred_element_type=WIDE)


def contract_rows(left, right):
    return lax.dot_general(
        left, right, (((0,), (0,)), ((), ())), preferred_element_type=WIDE
    )


def contract_cols(left, right):
    return lax.dot_general(
        left, right, (((1,), (1,)), ((), ())), preferred_element_type=WIDE
    )


def angles(segment_ids):
    length = segment_ids.shape[-1]
    before = jnp.sum(
        (segment_ids[:, None, :] < segment_ids[:, :, None]).astype(jnp.int32), axis=2
    )
    place = (jnp.arange(length, dtype=jnp.int32)[None] - before).astype(WIDE)
    half = HEAD_DIM // 2
    freqs = 10000.0 ** (-jnp.arange(half, dtype=WIDE) / half)
    turn = place[..., None] * freqs
    return (jnp.cos(turn), jnp.sin(turn))


def rotate(values, cosine, sine):
    half = values.shape[-1] // 2
    first = values[..., :half]
    second = values[..., half:]
    return jnp.concatenate(
        [first * cosine - second * sine, second * cosine + first * sine], axis=-1
    )


def norm_back(normed_grad, gain, unit, scale):
    scaled = normed_grad * gain[None, :]
    return scale * (scaled - unit * jnp.mean(scaled * unit, axis=1, keepdims=True))


PUMPS = (1, 2, 2, 2, 2, 2, 2, 1, 3, 0, 3, 4, 3, 1)


def tie(*values):
    return lax.optimization_barrier(values)


def late(values, *marks):
    return list(tie(*values, *marks))[: len(values)]


def blank(shape):
    return pl.pallas_call(
        lambda out: None,
        out_shape=jax.ShapeDtypeStruct(shape, WIDE),
        out_specs=pl.BlockSpec(memory_space=pl.ANY),
        name="blank",
    )()


def put(target, value, row, col):
    return lax.dynamic_update_slice(target, value.astype(target.dtype), (row, col))


class Flow:
    def __init__(self):
        self.tasks = []
        self.turn = 0

    def add(self, task):
        self.tasks.append((task, *next(task)))

    def advance(self, index, held):
        task = self.tasks[index][0]
        try:
            self.tasks[index] = (task, *task.send(held))
            self.turn = index + 1
            return self.tasks[index][2]
        except StopIteration:
            del self.tasks[index]
            self.turn = index
            return []

    def pump(self, times, *values):
        sent = []
        for _ in range(times):
            if not self.tasks:
                break
            index = self.turn % len(self.tasks)
            held = self.tasks[index][1]
            tied = tie(*values, *held)
            values = tied[: len(values)]
            sent += self.advance(index, tied[len(values) :])
        if sent:
            values = late(values, *sent)
        return values if len(values) != 1 else values[0]

    def beside(self, times, value):
        sent = []
        for _ in range(times):
            if not self.tasks:
                break
            index = self.turn % len(self.tasks)
            held = self.tasks[index][1]
            sent += self.advance(index, late(held, *sent) if sent else held)
        return late([value], *sent)[0] if sent else value

    def after(self, *marks):
        self.tasks = [(task, late(held, *marks), sent) for task, held, sent in self.tasks]

    def finish(self):
        while self.tasks:
            index = self.turn % len(self.tasks)
            self.advance(index, self.tasks[index][1])


class Ring:
    def __init__(self, mesh):
        self.shards = mesh.shape["shard"]
        self.reps = mesh.shape["rep"]
        self.line = self.reps // 2
        self.shard = lax.axis_index("shard")
        self.rep = lax.axis_index("rep")
        self.low = self.rep % 2
        self.high = self.rep // 2
        n = self.reps
        order = list(range(0, n, 2)) + list(range(n - 1, 0, -2))
        self.ways = [
            [(order[i], order[(i + step) % n]) for i in range(n)] for step in (1, -1)
        ]
        self.place = jnp.where(self.low == 0, self.high, n - 1 - self.high)

    def swap(self, value, k):
        return lax.ppermute(value, "shard", [(s, s ^ k) for s in range(self.shards)])

    def pair(self, value, k=1):
        return lax.ppermute(value, "rep", [(r, r ^ k) for r in range(self.reps)])

    def step(self, value, way):
        return lax.ppermute(value, "rep", self.ways[way])

    def gather(self, own):
        far = self.swap(own, 2)
        return [own, self.swap(own, 1), far, self.swap(far, 1)]

    def scatter(self, blocks, between=lambda v: v, flow=None):
        near = self.swap(jnp.concatenate([blocks[1], blocks[3]], axis=0), 1)
        n = blocks[0].shape[0]
        far = blocks[2] + near[n:]
        if flow is not None:
            flow.after(far)
        far = between(self.swap(far, 2))
        return blocks[0].astype(WIDE) + near[:n].astype(WIDE) + far.astype(WIDE)

    def ring_sum(self, chunk, between, store):
        n = self.reps
        signs = (-1, 1)

        def own(way, index):
            return chunk(way * n + lax.rem(index + 4 * n, n))

        parts = [own(way, self.place + signs[way]) for way in (0, 1)]
        for s in range(n - 1):
            got = yield [self.step(parts[way], way) for way in (0, 1)], parts
            parts = [got[way] + own(way, self.place + signs[way] * (s + 2)) for way in (0, 1)]
        now = yield from between(parts)
        for way in (0, 1):
            store(way, self.place, now[way])
        for s in range(n - 1):
            now = yield [self.step(now[way], way) for way in (0, 1)], now
            for way in (0, 1):
                at = lax.rem(self.place + signs[way] * (s + 1) + 4 * n, n)
                store(way, at, now[way])

    def exchange(self, parts, splits):
        count, rows, cols = parts[0].shape
        blocks = [
            [
                lax.dynamic_index_in_dim(part, self.shard ^ k, 0, keepdims=False)
                for part in parts
            ]
            for k in range(count)
        ]
        sent = [jnp.stack(blocks[k]) for k in range(1, count)]
        moved = yield [self.swap(item, k) for k, item in enumerate(sent, 1)], sent
        blocks[1:] = moved
        wholes = []
        for i in range(len(parts)):
            whole = jnp.zeros((rows, count * cols), parts[i].dtype)
            for k in range(count):
                for a, b in zip(splits, splits[1:]):
                    at = count * a + (self.shard ^ k) * (b - a)
                    whole = put(whole, blocks[k][i][:, a:b], 0, at)
            wholes.append(whole)
        return wholes


class Columns:
    def __init__(self, ring, weight, bits):
        self.ring = ring
        self.weight = weight
        self.rows = weight.shape[0]
        self.bits = bits
        self.size = self.rows >> len(bits)
        share = sum(((ring.rep // bit) % 2) << i for i, bit in enumerate(bits))
        pieces = [self.cols(k, share * self.size, self.size) for k in range(2, ring.shards)]
        self.got = [[ring.swap(piece, k)] for k, piece in enumerate(pieces, 2)]
        self.near = ring.swap(self.cols(1, 0, self.rows), 1)
        self.held = [share]

    def cols(self, k, start, size):
        part = self.weight.shape[1] // self.ring.shards
        return lax.dynamic_slice(self.weight, (start, (self.ring.shard ^ k) * part), (size, part))

    def settle(self, *values, only=None):
        for i in range(len(self.got)) if only is None else [only]:
            tied = tie(*values, *self.got[i])
            values, self.got[i] = tied[: len(values)], list(tied[len(values) :])
        return values if len(values) != 1 else values[0]

    def after(self, *marks):
        self.near, *_ = late([self.near], *marks)
        self.got = [late(pieces, *marks) for pieces in self.got]
        self.weight, *_ = late([self.weight], *marks)

    def trade(self, level):
        bit = self.bits[level]
        self.got = [
            pieces + [self.ring.pair(piece, bit) for piece in pieces] for pieces in self.got
        ]
        self.held = self.held + [at ^ (1 << level) for at in self.held]

    def whole(self):
        ring = self.ring
        whole = jnp.zeros((ring.shards * self.rows, self.near.shape[1]), self.near.dtype)
        whole = put(whole, self.cols(0, 0, self.rows), ring.shard * self.rows, 0)
        whole = put(whole, self.near, (ring.shard ^ 1) * self.rows, 0)
        for k, pieces in enumerate(self.got, 2):
            for at, piece in zip(self.held, pieces):
                whole = put(whole, piece, (ring.shard ^ k) * self.rows + at * self.size, 0)
        return whole


def shards(
    mesh,
    hidden_in,
    segments,
    cotangent,
    attn_gain,
    w_query,
    w_key,
    w_value,
    w_out,
    mlp_gain,
    w_gate,
    w_up,
    w_down,
):
    ring = Ring(mesh)
    flow = Flow()
    count = ring.shards
    reps = ring.reps
    own_low = hidden_in[0]
    length, width = own_low.shape
    group = HEADS // KV_HEADS
    block = group * HEAD_DIM
    tokens = count * length
    rows = width // count
    factor = 1.0 / math.sqrt(HEAD_DIM)

    hidden_blocks = ring.gather(own_low)
    segment_ids = jnp.concatenate(ring.gather(segments), axis=0)
    gains = jnp.stack([attn_gain, mlp_gain])
    gain_blocks = ring.gather(gains)
    whole_gain = jnp.zeros((2, width), gains.dtype)
    for k, piece in enumerate(gain_blocks):
        whole_gain = put(whole_gain, piece, 0, (ring.shard ^ k) * rows)
    gain1 = whole_gain[0].astype(WIDE)
    gain2 = whole_gain[1].astype(WIDE)
    w_kv = jnp.concatenate(
        [
            w_key.reshape(rows, count, HEAD_DIM),
            w_value.reshape(rows, count, HEAD_DIM),
        ],
        axis=2,
    ).reshape(rows, count * 2 * HEAD_DIM)
    query_cols = Columns(ring, w_query, ())
    kv_cols = Columns(ring, w_kv, ())
    hidden_blocks = query_cols.settle(*hidden_blocks)
    hidden_blocks = kv_cols.settle(*hidden_blocks)
    gate_cols = Columns(ring, w_gate, (2,))
    up_cols = Columns(ring, w_up, (1,))
    w_query_cols = query_cols.whole()
    w_kv_cols = kv_cols.whole()

    cosine, sine = angles(segment_ids)
    order = jnp.arange(length, dtype=jnp.int32)
    allowed = (
        (segment_ids[:, :, None] == segment_ids[:, None, :]) & (order[:, None] >= order[None, :])
    )[:, None]

    hidden_all = jnp.concatenate(hidden_blocks, axis=0).astype(WIDE)
    scale1_all = lax.rsqrt(jnp.mean(hidden_all * hidden_all, axis=1, keepdims=True) + EPS)
    normed1 = (hidden_all * scale1_all * gain1[None, :]).astype(LOW)

    query_raw = mm(normed1, w_query_cols)
    kv_raw = mm(normed1, w_kv_cols)
    cos_q, sin_q = cosine[:, :, None, :], sine[:, :, None, :]
    query = rotate(query_raw.reshape(count, length, group, HEAD_DIM), cos_q, sin_q).astype(LOW)
    keys = rotate(kv_raw[:, :HEAD_DIM].reshape(count, length, HEAD_DIM), cosine, sine).astype(LOW)
    values = kv_raw[:, HEAD_DIM:].reshape(count, length, HEAD_DIM).astype(LOW)
    query = gate_cols.settle(query)
    gate_cols.trade(0)

    raw = jnp.einsum("bqgd,bkd->bgqk", query, keys, preferred_element_type=WIDE) * factor
    masked = jnp.where(allowed, raw, -1000000000.0)
    peak = jnp.max(masked, axis=-1, keepdims=True)
    expo = jnp.exp(masked - peak)
    total = jnp.sum(expo, axis=-1, keepdims=True)
    probs = expo / total
    probs_low = probs.astype(LOW)
    log_total = peak + jnp.log(total)
    attended = (
        jnp.einsum("bgqk,bkd->bqgd", probs_low, values, preferred_element_type=WIDE)
        .reshape(tokens, block)
        .astype(LOW)
    )
    attended = gate_cols.settle(attended, only=0)
    out_part = up_cols.settle(mm(attended, w_out).astype(LOW)).reshape(count, length, width)
    up_cols.trade(0)
    reduced = ring.scatter(
        [out_part[k] for k in range(count)], gate_cols.settle
    )
    outs = {
        "query": blank(w_query.shape),
        "key": blank(w_key.shape),
        "value": blank(w_value.shape),
        "out": blank((rows, width)),
        "gate": blank(w_gate.shape),
        "up": blank(w_up.shape),
        "down": blank(w_down.shape),
    }
    hidden = own_low.astype(WIDE)
    middle = hidden + reduced
    scale2 = lax.rsqrt(jnp.mean(middle * middle, axis=1, keepdims=True) + EPS)
    unit2 = middle * scale2
    normed2_own = (unit2 * gain2[None, :]).astype(LOW)
    normed2_blocks = ring.gather(normed2_own)
    (upstream_own,) = late([cotangent[0]], normed2_blocks[2])
    upstream_far = ring.swap(upstream_own, 2)
    normed2 = jnp.concatenate(normed2_blocks, axis=0)

    ff_own = w_down.shape[0]
    gate_cols.after(normed2_own)
    up_cols.after(normed2_own)
    w_gate_cols = gate_cols.whole()
    w_up_cols = up_cols.whole()
    gate = mm(normed2, w_gate_cols)
    upward = mm(normed2, w_up_cols)
    sigmoid_gate = jax.nn.sigmoid(gate)
    silu_gate = gate * sigmoid_gate
    inner = (silu_gate * upward).astype(LOW)
    (upstream_far,) = late([upstream_far], inner)
    upstream_all = jnp.concatenate(
        [
            upstream_own,
            ring.swap(upstream_own, 1),
            upstream_far,
            ring.swap(upstream_far, 1),
        ],
        axis=0,
    )

    def unpack(names, widths, n):
        def store(way, index, value):
            at = 0
            for name, cols in zip(names, widths):
                piece = value[:, at : at + cols]
                outs[name] = put(outs[name], piece, (way * reps + index) * n, 0)
                at += cols

        return store

    def first_blocks(parts):
        yield from ()
        return [part[0] for part in parts]

    grad_down = contract_rows(inner, upstream_all).astype(LOW)
    def chunk_of(value, axis):
        n = value.shape[axis] // (2 * reps)
        return lambda index: lax.dynamic_slice_in_dim(value, index * n, n, axis)

    n_down = ff_own // (2 * reps)
    flow.add(
        ring.ring_sum(
            chunk_of(grad_down[None], 1), first_blocks, unpack(["down"], [width], n_down)
        )
    )
    upstream_next, grad_down = tie(upstream_all, grad_down)
    inner_grad = contract_cols(upstream_next, w_down)
    gate_grad = (inner_grad * upward * sigmoid_gate * (1.0 + gate * (1.0 - sigmoid_gate))).astype(
        LOW
    )
    up_grad = (inner_grad * silu_gate).astype(LOW)
    gate_grad, up_grad = flow.pump(1, gate_grad, up_grad)

    n_rows = rows // (2 * reps)
    fulls = []
    for cols in (gate_grad, up_grad):
        full = contract_rows(normed2, cols).astype(LOW).reshape(count, rows, ff_own)
        full, gate_grad, up_grad = flow.pump(PUMPS[0], full, gate_grad, up_grad)
        fulls.append(chunk_of(full, 1))
    flow.add(
        ring.ring_sum(
            lambda index: jnp.concatenate([full(index) for full in fulls], axis=2),
            lambda v: ring.exchange(v, (0, ff_own, 2 * ff_own)),
            unpack(["gate", "up"], [count * ff_own] * 2, n_rows),
        )
    )

    back_part = contract_cols(gate_grad, w_gate_cols)
    back_part, up_grad = flow.pump(PUMPS[13], back_part, up_grad)
    back_part = (back_part + contract_cols(up_grad, w_up_cols)).astype(LOW)
    back_part = flow.pump(PUMPS[1], back_part).reshape(count, length, width)
    normed2_grad = ring.scatter([back_part[k] for k in range(count)], lambda v: flow.beside(PUMPS[2], v), flow)

    grad_mlp_gain = jnp.sum(normed2_grad * unit2, axis=0)
    middle_grad = cotangent[0].astype(WIDE) + norm_back(normed2_grad, gain2, unit2, scale2)
    middle_low = middle_grad.astype(LOW)
    flow.after(middle_low)
    branch_far = flow.beside(PUMPS[3], ring.swap(middle_low, 2))
    branch_grad = jnp.concatenate(
        [middle_low, ring.swap(middle_low, 1), branch_far, ring.swap(branch_far, 1)], axis=0
    )
    attended_grad = (
        contract_cols(branch_grad, w_out).astype(LOW).reshape(count, length, group, HEAD_DIM)
    )
    attended_grad = flow.pump(PUMPS[4], attended_grad)
    probs = jnp.exp(masked - log_total)
    probs_grad = jnp.einsum("bqgd,bkd->bgqk", attended_grad, values, preferred_element_type=WIDE)
    inner_sum = jnp.sum(probs * probs_grad, axis=-1, keepdims=True)
    score_grad = (probs * (probs_grad - inner_sum)).astype(LOW)
    score_grad = flow.pump(PUMPS[5], score_grad)
    query_part = (
        jnp.einsum("bgqk,bkd->bqgd", score_grad, keys, preferred_element_type=WIDE) * factor
    )
    key_part = jnp.einsum("bgqk,bqgd->bkd", score_grad, query, preferred_element_type=WIDE) * factor
    value_part = jnp.einsum(
        "bgqk,bqgd->bkd", probs.astype(LOW), attended_grad, preferred_element_type=WIDE
    )
    query_grad = rotate(query_part, cos_q, -sin_q).astype(LOW).reshape(tokens, block)
    key_grad = rotate(key_part, cosine, -sine).astype(LOW).reshape(tokens, HEAD_DIM)
    value_grad = value_part.astype(LOW).reshape(tokens, HEAD_DIM)
    qkv_grad = jnp.concatenate([query_grad, key_grad, value_grad], axis=1)
    qkv_grad = flow.pump(PUMPS[6], qkv_grad)

    grad_qkv = contract_rows(normed1, qkv_grad).astype(LOW)
    grad_out = contract_rows(attended, branch_grad).astype(LOW)
    grad_qkv, grad_out, qkv_grad = flow.pump(PUMPS[7], grad_qkv, grad_out, qkv_grad)
    qkv_cols = qkv_grad.shape[1]
    qkv_chunk = chunk_of(grad_qkv.reshape(count, rows, qkv_cols), 1)
    out_chunk = chunk_of(grad_out, 0)

    def attn_chunk(index):
        out = jnp.transpose(out_chunk(index).reshape(n_rows, count, rows), (1, 0, 2))
        return jnp.concatenate([qkv_chunk(index), out], axis=2)

    def attn_message(parts):
        moved = yield from ring.exchange([part[:, :, :qkv_cols] for part in parts], (0, qkv_cols))
        ends = (0, block, block + HEAD_DIM, qkv_cols)
        moved = [
            jnp.concatenate(
                [
                    whole[:, s * qkv_cols + a : s * qkv_cols + b]
                    for a, b in zip(ends, ends[1:])
                    for s in range(count)
                ],
                axis=1,
            )
            for whole in moved
        ]
        still = [
            jnp.transpose(part[:, :, qkv_cols:], (1, 0, 2)).reshape(n_rows, width)
            for part in parts
        ]
        return [jnp.concatenate(both, axis=1) for both in zip(moved, still)]

    flow.add(
        ring.ring_sum(
            attn_chunk,
            attn_message,
            unpack(
                ["query", "key", "value", "out"],
                [w_query.shape[1], w_key.shape[1], w_value.shape[1], width],
                n_rows,
            ),
        )
    )

    qkv_grad = flow.pump(PUMPS[12], qkv_grad)
    back_part = (
        contract_cols(qkv_grad[:, :block], w_query_cols)
        + contract_cols(qkv_grad[:, block:], w_kv_cols)
    ).astype(LOW)
    back_part = flow.pump(1, back_part).reshape(count, length, width)
    normed1_grad = ring.scatter([back_part[k] for k in range(count)], lambda v: flow.beside(PUMPS[8], v), flow)
    scale1 = lax.rsqrt(jnp.mean(hidden * hidden, axis=1, keepdims=True) + EPS)
    unit1 = hidden * scale1
    grad_attn_gain = jnp.sum(normed1_grad * unit1, axis=0)
    input_grad = middle_grad + norm_back(normed1_grad, gain1, unit1, scale1)
    def gain_sum(both):
        k = 1
        while k < count:
            (got,) = yield [ring.swap(both, k)], [both]
            both = both + got
            k *= 2
        both = lax.dynamic_slice_in_dim(both, ring.shard * rows, rows, 1)
        k = 1
        while k < reps:
            (got,) = yield [ring.pair(both, k)], [both]
            both = both + got
            k *= 2
        outs["gains"] = both

    flow.add(gain_sum(jnp.stack([grad_attn_gain, grad_mlp_gain])))
    (inner,) = late([inner], input_grad)

    down_part = mm(inner, w_down).astype(LOW)
    down_part = flow.pump(PUMPS[10], down_part).reshape(count, length, width)
    layer_out = (
        middle + ring.scatter([down_part[k] for k in range(count)], lambda v: flow.beside(PUMPS[11], v), flow)
    ).astype(LOW)

    flow.finish()
    mine = outs["gains"]

    return (
        layer_out[None],
        input_grad[None],
        mine[0],
        outs["query"],
        outs["key"],
        outs["value"],
        outs["out"],
        mine[1],
        outs["gate"],
        outs["up"],
        outs["down"],
    )


def solution(mesh):
    both = ("shard", "rep")
    row, vec = P("shard", None), P("shard")
    act = P(both, None, None)
    in_specs = (act, P(both, None), act, vec, row, row, row, row, vec, row, row, row)
    out_specs = (act, act, vec, row, row, row, row, vec, row, row, row)

    def body(*args):
        return shards(mesh, *args)

    return jax.shard_map(
        body, mesh=mesh, in_specs=in_specs, out_specs=out_specs, check_vma=False
    )
```

```python
import math

import jax
import jax.numpy as jnp
from jax import lax
from jax.experimental import pallas as pl
from jax.sharding import PartitionSpec as P

HEADS = 32
KV_HEADS = 4
HEAD_DIM = 64
EPS = 1e-05
LOW = jnp.bfloat16
WIDE = jnp.float32


def mm(left, right):
    return jnp.dot(left, right, preferred_element_type=WIDE)


def contract_rows(left, right):
    return lax.dot_general(
        left, right, (((0,), (0,)), ((), ())), preferred_element_type=WIDE
    )


def contract_cols(left, right):
    return lax.dot_general(
        left, right, (((1,), (1,)), ((), ())), preferred_element_type=WIDE
    )


def angles(segment_ids):
    length = segment_ids.shape[-1]
    before = jnp.sum(
        (segment_ids[:, None, :] < segment_ids[:, :, None]).astype(jnp.int32), axis=2
    )
    place = (jnp.arange(length, dtype=jnp.int32)[None] - before).astype(WIDE)
    half = HEAD_DIM // 2
    freqs = 10000.0 ** (-jnp.arange(half, dtype=WIDE) / half)
    turn = place[..., None] * freqs
    return (jnp.cos(turn), jnp.sin(turn))


def rotate(values, cosine, sine):
    half = values.shape[-1] // 2
    first = values[..., :half]
    second = values[..., half:]
    return jnp.concatenate(
        [first * cosine - second * sine, second * cosine + first * sine], axis=-1
    )


def norm_back(normed_grad, gain, unit, scale):
    scaled = normed_grad * gain[None, :]
    return scale * (scaled - unit * jnp.mean(scaled * unit, axis=1, keepdims=True))


PUMPS = (1, 2, 2, 2, 1, 2, 2, 1, 3, 0, 3, 4, 3, 1)


def tie(*values):
    return lax.optimization_barrier(values)


def late(values, *marks):
    return list(tie(*values, *marks))[: len(values)]


def blank(shape):
    return pl.pallas_call(
        lambda out: None,
        out_shape=jax.ShapeDtypeStruct(shape, WIDE),
        out_specs=pl.BlockSpec(memory_space=pl.ANY),
        name="blank",
    )()


def put(target, value, row, col):
    return lax.dynamic_update_slice(target, value.astype(target.dtype), (row, col))


class Flow:
    def __init__(self):
        self.tasks = []
        self.turn = 0

    def add(self, task):
        self.tasks.append((task, *next(task)))

    def advance(self, index, held):
        task = self.tasks[index][0]
        try:
            self.tasks[index] = (task, *task.send(held))
            self.turn = index + 1
            return self.tasks[index][2]
        except StopIteration:
            del self.tasks[index]
            self.turn = index
            return []

    def pump(self, times, *values):
        sent = []
        for _ in range(times):
            if not self.tasks:
                break
            index = self.turn % len(self.tasks)
            held = self.tasks[index][1]
            tied = tie(*values, *held)
            values = tied[: len(values)]
            sent += self.advance(index, tied[len(values) :])
        if sent:
            values = late(values, *sent)
        return values if len(values) != 1 else values[0]

    def beside(self, times, value):
        sent = []
        for _ in range(times):
            if not self.tasks:
                break
            index = self.turn % len(self.tasks)
            held = self.tasks[index][1]
            sent += self.advance(index, late(held, *sent) if sent else held)
        return late([value], *sent)[0] if sent else value

    def after(self, *marks):
        self.tasks = [(task, late(held, *marks), sent) for task, held, sent in self.tasks]

    def finish(self):
        while self.tasks:
            index = self.turn % len(self.tasks)
            self.advance(index, self.tasks[index][1])


class Ring:
    def __init__(self, mesh):
        self.shards = mesh.shape["shard"]
        self.reps = mesh.shape["rep"]
        self.line = self.reps // 2
        self.shard = lax.axis_index("shard")
        self.rep = lax.axis_index("rep")
        self.low = self.rep % 2
        self.high = self.rep // 2
        n = self.reps
        order = list(range(0, n, 2)) + list(range(n - 1, 0, -2))
        self.ways = [
            [(order[i], order[(i + step) % n]) for i in range(n)] for step in (1, -1)
        ]
        self.place = jnp.where(self.low == 0, self.high, n - 1 - self.high)

    def swap(self, value, k):
        return lax.ppermute(value, "shard", [(s, s ^ k) for s in range(self.shards)])

    def pair(self, value, k=1):
        return lax.ppermute(value, "rep", [(r, r ^ k) for r in range(self.reps)])

    def step(self, value, way):
        return lax.ppermute(value, "rep", self.ways[way])

    def gather(self, own):
        far = self.swap(own, 2)
        return [own, self.swap(own, 1), far, self.swap(far, 1)]

    def scatter(self, blocks, between=lambda v: v, flow=None):
        near = self.swap(jnp.concatenate([blocks[1], blocks[3]], axis=0), 1)
        n = blocks[0].shape[0]
        far = blocks[2] + near[n:]
        if flow is not None:
            flow.after(far)
        far = between(self.swap(far, 2))
        return blocks[0].astype(WIDE) + near[:n].astype(WIDE) + far.astype(WIDE)

    def ring_sum(self, chunk, between, store):
        n = self.reps
        signs = (-1, 1)

        def own(way, index):
            return chunk(way * n + lax.rem(index + 4 * n, n))

        parts = [own(way, self.place + signs[way]) for way in (0, 1)]
        for s in range(n - 1):
            got = yield [self.step(parts[way], way) for way in (0, 1)], parts
            parts = [got[way] + own(way, self.place + signs[way] * (s + 2)) for way in (0, 1)]
        now = yield from between(parts)
        for way in (0, 1):
            store(way, self.place, now[way])
        for s in range(n - 1):
            now = yield [self.step(now[way], way) for way in (0, 1)], now
            for way in (0, 1):
                at = lax.rem(self.place + signs[way] * (s + 1) + 4 * n, n)
                store(way, at, now[way])

    def exchange(self, parts, splits):
        count, rows, cols = parts[0].shape
        blocks = [
            [
                lax.dynamic_index_in_dim(part, self.shard ^ k, 0, keepdims=False)
                for part in parts
            ]
            for k in range(count)
        ]
        sent = [jnp.stack(blocks[k]) for k in range(1, count)]
        moved = yield [self.swap(item, k) for k, item in enumerate(sent, 1)], sent
        blocks[1:] = moved
        wholes = []
        for i in range(len(parts)):
            whole = jnp.zeros((rows, count * cols), parts[i].dtype)
            for k in range(count):
                for a, b in zip(splits, splits[1:]):
                    at = count * a + (self.shard ^ k) * (b - a)
                    whole = put(whole, blocks[k][i][:, a:b], 0, at)
            wholes.append(whole)
        return wholes


class Columns:
    def __init__(self, ring, weight, bits):
        self.ring = ring
        self.weight = weight
        self.rows = weight.shape[0]
        self.bits = bits
        self.size = self.rows >> len(bits)
        share = sum(((ring.rep // bit) % 2) << i for i, bit in enumerate(bits))
        pieces = [self.cols(k, share * self.size, self.size) for k in range(2, ring.shards)]
        self.got = [[ring.swap(piece, k)] for k, piece in enumerate(pieces, 2)]
        self.near = ring.swap(self.cols(1, 0, self.rows), 1)
        self.held = [share]

    def cols(self, k, start, size):
        part = self.weight.shape[1] // self.ring.shards
        return lax.dynamic_slice(self.weight, (start, (self.ring.shard ^ k) * part), (size, part))

    def settle(self, *values, only=None):
        for i in range(len(self.got)) if only is None else [only]:
            tied = tie(*values, *self.got[i])
            values, self.got[i] = tied[: len(values)], list(tied[len(values) :])
        return values if len(values) != 1 else values[0]

    def after(self, *marks):
        self.near, *_ = late([self.near], *marks)
        self.got = [late(pieces, *marks) for pieces in self.got]
        self.weight, *_ = late([self.weight], *marks)

    def trade(self, level):
        bit = self.bits[level]
        self.got = [
            pieces + [self.ring.pair(piece, bit) for piece in pieces] for pieces in self.got
        ]
        self.held = self.held + [at ^ (1 << level) for at in self.held]

    def whole(self):
        ring = self.ring
        whole = jnp.zeros((ring.shards * self.rows, self.near.shape[1]), self.near.dtype)
        whole = put(whole, self.cols(0, 0, self.rows), ring.shard * self.rows, 0)
        whole = put(whole, self.near, (ring.shard ^ 1) * self.rows, 0)
        for k, pieces in enumerate(self.got, 2):
            for at, piece in zip(self.held, pieces):
                whole = put(whole, piece, (ring.shard ^ k) * self.rows + at * self.size, 0)
        return whole


def shards(
    mesh,
    hidden_in,
    segments,
    cotangent,
    attn_gain,
    w_query,
    w_key,
    w_value,
    w_out,
    mlp_gain,
    w_gate,
    w_up,
    w_down,
):
    ring = Ring(mesh)
    flow = Flow()
    count = ring.shards
    reps = ring.reps
    own_low = hidden_in[0]
    length, width = own_low.shape
    group = HEADS // KV_HEADS
    block = group * HEAD_DIM
    tokens = count * length
    rows = width // count
    factor = 1.0 / math.sqrt(HEAD_DIM)

    hidden_blocks = ring.gather(own_low)
    segment_ids = jnp.concatenate(ring.gather(segments), axis=0)
    gains = jnp.stack([attn_gain, mlp_gain])
    gain_blocks = ring.gather(gains)
    whole_gain = jnp.zeros((2, width), gains.dtype)
    for k, piece in enumerate(gain_blocks):
        whole_gain = put(whole_gain, piece, 0, (ring.shard ^ k) * rows)
    gain1 = whole_gain[0].astype(WIDE)
    gain2 = whole_gain[1].astype(WIDE)
    w_kv = jnp.concatenate(
        [
            w_key.reshape(rows, count, HEAD_DIM),
            w_value.reshape(rows, count, HEAD_DIM),
        ],
        axis=2,
    ).reshape(rows, count * 2 * HEAD_DIM)
    query_cols = Columns(ring, w_query, ())
    kv_cols = Columns(ring, w_kv, ())
    hidden_blocks = query_cols.settle(*hidden_blocks)
    hidden_blocks = kv_cols.settle(*hidden_blocks)
    gate_cols = Columns(ring, w_gate, (2,))
    up_cols = Columns(ring, w_up, (1,))
    w_query_cols = query_cols.whole()
    w_kv_cols = kv_cols.whole()

    cosine, sine = angles(segment_ids)
    order = jnp.arange(length, dtype=jnp.int32)
    allowed = (
        (segment_ids[:, :, None] == segment_ids[:, None, :]) & (order[:, None] >= order[None, :])
    )[:, None]

    hidden_all = jnp.concatenate(hidden_blocks, axis=0).astype(WIDE)
    scale1_all = lax.rsqrt(jnp.mean(hidden_all * hidden_all, axis=1, keepdims=True) + EPS)
    normed1 = (hidden_all * scale1_all * gain1[None, :]).astype(LOW)

    query_raw = mm(normed1, w_query_cols)
    kv_raw = mm(normed1, w_kv_cols)
    cos_q, sin_q = cosine[:, :, None, :], sine[:, :, None, :]
    query = rotate(query_raw.reshape(count, length, group, HEAD_DIM), cos_q, sin_q).astype(LOW)
    keys = rotate(kv_raw[:, :HEAD_DIM].reshape(count, length, HEAD_DIM), cosine, sine).astype(LOW)
    values = kv_raw[:, HEAD_DIM:].reshape(count, length, HEAD_DIM).astype(LOW)
    query = gate_cols.settle(query)
    gate_cols.trade(0)

    raw = jnp.einsum("bqgd,bkd->bgqk", query, keys, preferred_element_type=WIDE) * factor
    masked = jnp.where(allowed, raw, -1000000000.0)
    peak = jnp.max(masked, axis=-1, keepdims=True)
    expo = jnp.exp(masked - peak)
    total = jnp.sum(expo, axis=-1, keepdims=True)
    probs = expo / total
    probs_low = probs.astype(LOW)
    log_total = peak + jnp.log(total)
    attended = (
        jnp.einsum("bgqk,bkd->bqgd", probs_low, values, preferred_element_type=WIDE)
        .reshape(tokens, block)
        .astype(LOW)
    )
    attended = gate_cols.settle(attended, only=0)
    out_part = up_cols.settle(mm(attended, w_out).astype(LOW)).reshape(count, length, width)
    up_cols.trade(0)
    reduced = ring.scatter(
        [out_part[k] for k in range(count)], gate_cols.settle
    )
    outs = {
        "query": blank(w_query.shape),
        "key": blank(w_key.shape),
        "value": blank(w_value.shape),
        "out": blank((rows, width)),
        "gate": blank(w_gate.shape),
        "up": blank(w_up.shape),
        "down": blank(w_down.shape),
    }
    hidden = own_low.astype(WIDE)
    middle = hidden + reduced
    scale2 = lax.rsqrt(jnp.mean(middle * middle, axis=1, keepdims=True) + EPS)
    unit2 = middle * scale2
    normed2_own = (unit2 * gain2[None, :]).astype(LOW)
    normed2_blocks = ring.gather(normed2_own)
    (upstream_own,) = late([cotangent[0]], normed2_blocks[2])
    upstream_far = ring.swap(upstream_own, 2)
    normed2 = jnp.concatenate(normed2_blocks, axis=0)

    ff_own = w_down.shape[0]
    gate_cols.after(normed2_own)
    up_cols.after(normed2_own)
    w_gate_cols = gate_cols.whole()
    w_up_cols = up_cols.whole()
    gate = mm(normed2, w_gate_cols)
    upward = mm(normed2, w_up_cols)
    sigmoid_gate = jax.nn.sigmoid(gate)
    silu_gate = gate * sigmoid_gate
    inner = (silu_gate * upward).astype(LOW)
    (upstream_far,) = late([upstream_far], inner)
    upstream_all = jnp.concatenate(
        [
            upstream_own,
            ring.swap(upstream_own, 1),
            upstream_far,
            ring.swap(upstream_far, 1),
        ],
        axis=0,
    )

    def unpack(names, widths, n):
        def store(way, index, value):
            at = 0
            for name, cols in zip(names, widths):
                piece = value[:, at : at + cols]
                outs[name] = put(outs[name], piece, (way * reps + index) * n, 0)
                at += cols

        return store

    def first_blocks(parts):
        yield from ()
        return [part[0] for part in parts]

    grad_down = contract_rows(inner, upstream_all).astype(LOW)
    def chunk_of(value, axis):
        n = value.shape[axis] // (2 * reps)
        return lambda index: lax.dynamic_slice_in_dim(value, index * n, n, axis)

    n_down = ff_own // (2 * reps)
    flow.add(
        ring.ring_sum(
            chunk_of(grad_down[None], 1), first_blocks, unpack(["down"], [width], n_down)
        )
    )
    upstream_next, grad_down = tie(upstream_all, grad_down)
    inner_grad = contract_cols(upstream_next, w_down)
    gate_grad = (inner_grad * upward * sigmoid_gate * (1.0 + gate * (1.0 - sigmoid_gate))).astype(
        LOW
    )
    up_grad = (inner_grad * silu_gate).astype(LOW)
    gate_grad, up_grad = flow.pump(1, gate_grad, up_grad)

    n_rows = rows // (2 * reps)
    fulls = []
    for cols in (gate_grad, up_grad):
        full = contract_rows(normed2, cols).astype(LOW).reshape(count, rows, ff_own)
        full, gate_grad, up_grad = flow.pump(PUMPS[0], full, gate_grad, up_grad)
        fulls.append(chunk_of(full, 1))
    flow.add(
        ring.ring_sum(
            lambda index: jnp.concatenate([full(index) for full in fulls], axis=2),
            lambda v: ring.exchange(v, (0, ff_own, 2 * ff_own)),
            unpack(["gate", "up"], [count * ff_own] * 2, n_rows),
        )
    )

    back_part = contract_cols(gate_grad, w_gate_cols)
    back_part, up_grad = flow.pump(PUMPS[13], back_part, up_grad)
    back_part = (back_part + contract_cols(up_grad, w_up_cols)).astype(LOW)
    back_part = flow.pump(PUMPS[1], back_part).reshape(count, length, width)
    normed2_grad = ring.scatter([back_part[k] for k in range(count)], lambda v: flow.beside(PUMPS[2], v), flow)

    grad_mlp_gain = jnp.sum(normed2_grad * unit2, axis=0)
    middle_grad = cotangent[0].astype(WIDE) + norm_back(normed2_grad, gain2, unit2, scale2)
    middle_low = middle_grad.astype(LOW)
    flow.after(middle_low)
    branch_far = flow.beside(PUMPS[3], ring.swap(middle_low, 2))
    branch_grad = jnp.concatenate(
        [middle_low, ring.swap(middle_low, 1), branch_far, ring.swap(branch_far, 1)], axis=0
    )
    attended_grad = (
        contract_cols(branch_grad, w_out).astype(LOW).reshape(count, length, group, HEAD_DIM)
    )
    attended_grad = flow.pump(PUMPS[4], attended_grad)
    probs = jnp.exp(masked - log_total)
    probs_grad = jnp.einsum("bqgd,bkd->bgqk", attended_grad, values, preferred_element_type=WIDE)
    inner_sum = jnp.sum(probs * probs_grad, axis=-1, keepdims=True)
    score_grad = (probs * (probs_grad - inner_sum)).astype(LOW)
    score_grad = flow.pump(PUMPS[5], score_grad)
    query_part = (
        jnp.einsum("bgqk,bkd->bqgd", score_grad, keys, preferred_element_type=WIDE) * factor
    )
    key_part = jnp.einsum("bgqk,bqgd->bkd", score_grad, query, preferred_element_type=WIDE) * factor
    value_part = jnp.einsum(
        "bgqk,bqgd->bkd", probs.astype(LOW), attended_grad, preferred_element_type=WIDE
    )
    query_grad = rotate(query_part, cos_q, -sin_q).astype(LOW).reshape(tokens, block)
    key_grad = rotate(key_part, cosine, -sine).astype(LOW).reshape(tokens, HEAD_DIM)
    value_grad = value_part.astype(LOW).reshape(tokens, HEAD_DIM)
    qkv_grad = jnp.concatenate([query_grad, key_grad, value_grad], axis=1)
    qkv_grad = flow.pump(PUMPS[6], qkv_grad)

    grad_qkv = contract_rows(normed1, qkv_grad).astype(LOW)
    grad_out = contract_rows(attended, branch_grad).astype(LOW)
    grad_qkv, grad_out, qkv_grad = flow.pump(PUMPS[7], grad_qkv, grad_out, qkv_grad)
    qkv_cols = qkv_grad.shape[1]
    qkv_chunk = chunk_of(grad_qkv.reshape(count, rows, qkv_cols), 1)
    out_chunk = chunk_of(grad_out, 0)

    def attn_chunk(index):
        out = jnp.transpose(out_chunk(index).reshape(n_rows, count, rows), (1, 0, 2))
        return jnp.concatenate([qkv_chunk(index), out], axis=2)

    def attn_message(parts):
        moved = yield from ring.exchange([part[:, :, :qkv_cols] for part in parts], (0, qkv_cols))
        ends = (0, block, block + HEAD_DIM, qkv_cols)
        moved = [
            jnp.concatenate(
                [
                    whole[:, s * qkv_cols + a : s * qkv_cols + b]
                    for a, b in zip(ends, ends[1:])
                    for s in range(count)
                ],
                axis=1,
            )
            for whole in moved
        ]
        still = [
            jnp.transpose(part[:, :, qkv_cols:], (1, 0, 2)).reshape(n_rows, width)
            for part in parts
        ]
        return [jnp.concatenate(both, axis=1) for both in zip(moved, still)]

    flow.add(
        ring.ring_sum(
            attn_chunk,
            attn_message,
            unpack(
                ["query", "key", "value", "out"],
                [w_query.shape[1], w_key.shape[1], w_value.shape[1], width],
                n_rows,
            ),
        )
    )

    qkv_grad = flow.pump(PUMPS[12], qkv_grad)
    back_part = (
        contract_cols(qkv_grad[:, :block], w_query_cols)
        + contract_cols(qkv_grad[:, block:], w_kv_cols)
    ).astype(LOW)
    back_part = flow.pump(1, back_part).reshape(count, length, width)
    normed1_grad = ring.scatter([back_part[k] for k in range(count)], lambda v: flow.beside(PUMPS[8], v), flow)
    scale1 = lax.rsqrt(jnp.mean(hidden * hidden, axis=1, keepdims=True) + EPS)
    unit1 = hidden * scale1
    grad_attn_gain = jnp.sum(normed1_grad * unit1, axis=0)
    input_grad = middle_grad + norm_back(normed1_grad, gain1, unit1, scale1)
    def gain_sum(both):
        k = 1
        while k < count:
            (got,) = yield [ring.swap(both, k)], [both]
            both = both + got
            k *= 2
        both = lax.dynamic_slice_in_dim(both, ring.shard * rows, rows, 1)
        k = 1
        while k < reps:
            (got,) = yield [ring.pair(both, k)], [both]
            both = both + got
            k *= 2
        outs["gains"] = both

    flow.add(gain_sum(jnp.stack([grad_attn_gain, grad_mlp_gain])))
    (inner,) = late([inner], input_grad)

    down_part = mm(inner, w_down).astype(LOW)
    down_part = flow.pump(PUMPS[10], down_part).reshape(count, length, width)
    layer_out = (
        middle + ring.scatter([down_part[k] for k in range(count)], lambda v: flow.beside(PUMPS[11], v), flow)
    ).astype(LOW)

    flow.finish()
    mine = outs["gains"]

    return (
        layer_out[None],
        input_grad[None],
        mine[0],
        outs["query"],
        outs["key"],
        outs["value"],
        outs["out"],
        mine[1],
        outs["gate"],
        outs["up"],
        outs["down"],
    )


def solution(mesh):
    both = ("shard", "rep")
    row, vec = P("shard", None), P("shard")
    act = P(both, None, None)
    in_specs = (act, P(both, None), act, vec, row, row, row, row, vec, row, row, row)
    out_specs = (act, act, vec, row, row, row, row, vec, row, row, row)

    def body(*args):
        return shards(mesh, *args)

    return jax.shard_map(
        body, mesh=mesh, in_specs=in_specs, out_specs=out_specs, check_vma=False
    )
```

```python
import math

import jax
import jax.numpy as jnp
from jax import lax
from jax.experimental import pallas as pl
from jax.sharding import PartitionSpec as P

HEADS = 32
KV_HEADS = 4
HEAD_DIM = 64
EPS = 1e-05
LOW = jnp.bfloat16
WIDE = jnp.float32


def mm(left, right):
    return jnp.dot(left, right, preferred_element_type=WIDE)


def contract_rows(left, right):
    return lax.dot_general(
        left, right, (((0,), (0,)), ((), ())), preferred_element_type=WIDE
    )


def contract_cols(left, right):
    return lax.dot_general(
        left, right, (((1,), (1,)), ((), ())), preferred_element_type=WIDE
    )


def angles(segment_ids):
    length = segment_ids.shape[-1]
    before = jnp.sum(
        (segment_ids[:, None, :] < segment_ids[:, :, None]).astype(jnp.int32), axis=2
    )
    place = (jnp.arange(length, dtype=jnp.int32)[None] - before).astype(WIDE)
    half = HEAD_DIM // 2
    freqs = 10000.0 ** (-jnp.arange(half, dtype=WIDE) / half)
    turn = place[..., None] * freqs
    return (jnp.cos(turn), jnp.sin(turn))


def rotate(values, cosine, sine):
    half = values.shape[-1] // 2
    first = values[..., :half]
    second = values[..., half:]
    return jnp.concatenate(
        [first * cosine - second * sine, second * cosine + first * sine], axis=-1
    )


def norm_back(normed_grad, gain, unit, scale):
    scaled = normed_grad * gain[None, :]
    return scale * (scaled - unit * jnp.mean(scaled * unit, axis=1, keepdims=True))


PUMPS = (1, 2, 2, 2, 1, 2, 2, 1, 2, 0, 3, 4, 3, 1)


def tie(*values):
    return lax.optimization_barrier(values)


def late(values, *marks):
    return list(tie(*values, *marks))[: len(values)]


def blank(shape):
    return pl.pallas_call(
        lambda out: None,
        out_shape=jax.ShapeDtypeStruct(shape, WIDE),
        out_specs=pl.BlockSpec(memory_space=pl.ANY),
        name="blank",
    )()


def put(target, value, row, col):
    return lax.dynamic_update_slice(target, value.astype(target.dtype), (row, col))


class Flow:
    def __init__(self):
        self.tasks = []
        self.turn = 0

    def add(self, task):
        self.tasks.append((task, *next(task)))

    def advance(self, index, held):
        task = self.tasks[index][0]
        try:
            self.tasks[index] = (task, *task.send(held))
            self.turn = index + 1
            return self.tasks[index][2]
        except StopIteration:
            del self.tasks[index]
            self.turn = index
            return []

    def pump(self, times, *values):
        sent = []
        for _ in range(times):
            if not self.tasks:
                break
            index = self.turn % len(self.tasks)
            held = self.tasks[index][1]
            tied = tie(*values, *held)
            values = tied[: len(values)]
            sent += self.advance(index, tied[len(values) :])
        if sent:
            values = late(values, *sent)
        return values if len(values) != 1 else values[0]

    def beside(self, times, value):
        sent = []
        for _ in range(times):
            if not self.tasks:
                break
            index = self.turn % len(self.tasks)
            held = self.tasks[index][1]
            sent += self.advance(index, late(held, *sent) if sent else held)
        return late([value], *sent)[0] if sent else value

    def after(self, *marks):
        self.tasks = [(task, late(held, *marks), sent) for task, held, sent in self.tasks]

    def finish(self):
        while self.tasks:
            index = self.turn % len(self.tasks)
            self.advance(index, self.tasks[index][1])


class Ring:
    def __init__(self, mesh):
        self.shards = mesh.shape["shard"]
        self.reps = mesh.shape["rep"]
        self.line = self.reps // 2
        self.shard = lax.axis_index("shard")
        self.rep = lax.axis_index("rep")
        self.low = self.rep % 2
        self.high = self.rep // 2
        n = self.reps
        order = list(range(0, n, 2)) + list(range(n - 1, 0, -2))
        self.ways = [
            [(order[i], order[(i + step) % n]) for i in range(n)] for step in (1, -1)
        ]
        self.place = jnp.where(self.low == 0, self.high, n - 1 - self.high)

    def swap(self, value, k):
        return lax.ppermute(value, "shard", [(s, s ^ k) for s in range(self.shards)])

    def pair(self, value, k=1):
        return lax.ppermute(value, "rep", [(r, r ^ k) for r in range(self.reps)])

    def step(self, value, way):
        return lax.ppermute(value, "rep", self.ways[way])

    def gather(self, own):
        far = self.swap(own, 2)
        return [own, self.swap(own, 1), far, self.swap(far, 1)]

    def scatter(self, blocks, between=lambda v: v, flow=None):
        near = self.swap(jnp.concatenate([blocks[1], blocks[3]], axis=0), 1)
        n = blocks[0].shape[0]
        far = blocks[2] + near[n:]
        if flow is not None:
            flow.after(far)
        far = between(self.swap(far, 2))
        return blocks[0].astype(WIDE) + near[:n].astype(WIDE) + far.astype(WIDE)

    def ring_sum(self, chunk, between, store):
        n = self.reps
        signs = (-1, 1)

        def own(way, index):
            return chunk(way * n + lax.rem(index + 4 * n, n))

        parts = [own(way, self.place + signs[way]) for way in (0, 1)]
        for s in range(n - 1):
            got = yield [self.step(parts[way], way) for way in (0, 1)], parts
            parts = [got[way] + own(way, self.place + signs[way] * (s + 2)) for way in (0, 1)]
        now = yield from between(parts)
        for way in (0, 1):
            store(way, self.place, now[way])
        for s in range(n - 1):
            now = yield [self.step(now[way], way) for way in (0, 1)], now
            for way in (0, 1):
                at = lax.rem(self.place + signs[way] * (s + 1) + 4 * n, n)
                store(way, at, now[way])

    def exchange(self, parts, splits):
        count, rows, cols = parts[0].shape
        blocks = [
            [
                lax.dynamic_index_in_dim(part, self.shard ^ k, 0, keepdims=False)
                for part in parts
            ]
            for k in range(count)
        ]
        sent = [jnp.stack(blocks[k]) for k in range(1, count)]
        moved = yield [self.swap(item, k) for k, item in enumerate(sent, 1)], sent
        blocks[1:] = moved
        wholes = []
        for i in range(len(parts)):
            whole = jnp.zeros((rows, count * cols), parts[i].dtype)
            for k in range(count):
                for a, b in zip(splits, splits[1:]):
                    at = count * a + (self.shard ^ k) * (b - a)
                    whole = put(whole, blocks[k][i][:, a:b], 0, at)
            wholes.append(whole)
        return wholes


class Columns:
    def __init__(self, ring, weight, bits):
        self.ring = ring
        self.weight = weight
        self.rows = weight.shape[0]
        self.bits = bits
        self.size = self.rows >> len(bits)
        share = sum(((ring.rep // bit) % 2) << i for i, bit in enumerate(bits))
        pieces = [self.cols(k, share * self.size, self.size) for k in range(2, ring.shards)]
        self.got = [[ring.swap(piece, k)] for k, piece in enumerate(pieces, 2)]
        self.near = ring.swap(self.cols(1, 0, self.rows), 1)
        self.held = [share]

    def cols(self, k, start, size):
        part = self.weight.shape[1] // self.ring.shards
        return lax.dynamic_slice(self.weight, (start, (self.ring.shard ^ k) * part), (size, part))

    def settle(self, *values, only=None):
        for i in range(len(self.got)) if only is None else [only]:
            tied = tie(*values, *self.got[i])
            values, self.got[i] = tied[: len(values)], list(tied[len(values) :])
        return values if len(values) != 1 else values[0]

    def after(self, *marks):
        self.near, *_ = late([self.near], *marks)
        self.got = [late(pieces, *marks) for pieces in self.got]
        self.weight, *_ = late([self.weight], *marks)

    def trade(self, level):
        bit = self.bits[level]
        self.got = [
            pieces + [self.ring.pair(piece, bit) for piece in pieces] for pieces in self.got
        ]
        self.held = self.held + [at ^ (1 << level) for at in self.held]

    def whole(self):
        ring = self.ring
        whole = jnp.zeros((ring.shards * self.rows, self.near.shape[1]), self.near.dtype)
        whole = put(whole, self.cols(0, 0, self.rows), ring.shard * self.rows, 0)
        whole = put(whole, self.near, (ring.shard ^ 1) * self.rows, 0)
        for k, pieces in enumerate(self.got, 2):
            for at, piece in zip(self.held, pieces):
                whole = put(whole, piece, (ring.shard ^ k) * self.rows + at * self.size, 0)
        return whole


def shards(
    mesh,
    hidden_in,
    segments,
    cotangent,
    attn_gain,
    w_query,
    w_key,
    w_value,
    w_out,
    mlp_gain,
    w_gate,
    w_up,
    w_down,
):
    ring = Ring(mesh)
    flow = Flow()
    count = ring.shards
    reps = ring.reps
    own_low = hidden_in[0]
    length, width = own_low.shape
    group = HEADS // KV_HEADS
    block = group * HEAD_DIM
    tokens = count * length
    rows = width // count
    factor = 1.0 / math.sqrt(HEAD_DIM)

    hidden_blocks = ring.gather(own_low)
    segment_ids = jnp.concatenate(ring.gather(segments), axis=0)
    gains = jnp.stack([attn_gain, mlp_gain])
    gain_blocks = ring.gather(gains)
    whole_gain = jnp.zeros((2, width), gains.dtype)
    for k, piece in enumerate(gain_blocks):
        whole_gain = put(whole_gain, piece, 0, (ring.shard ^ k) * rows)
    gain1 = whole_gain[0].astype(WIDE)
    gain2 = whole_gain[1].astype(WIDE)
    w_kv = jnp.concatenate(
        [
            w_key.reshape(rows, count, HEAD_DIM),
            w_value.reshape(rows, count, HEAD_DIM),
        ],
        axis=2,
    ).reshape(rows, count * 2 * HEAD_DIM)
    query_cols = Columns(ring, w_query, ())
    kv_cols = Columns(ring, w_kv, ())
    hidden_blocks = query_cols.settle(*hidden_blocks)
    hidden_blocks = kv_cols.settle(*hidden_blocks)
    gate_cols = Columns(ring, w_gate, (2,))
    up_cols = Columns(ring, w_up, (1,))
    w_query_cols = query_cols.whole()
    w_kv_cols = kv_cols.whole()

    cosine, sine = angles(segment_ids)
    order = jnp.arange(length, dtype=jnp.int32)
    allowed = (
        (segment_ids[:, :, None] == segment_ids[:, None, :]) & (order[:, None] >= order[None, :])
    )[:, None]

    hidden_all = jnp.concatenate(hidden_blocks, axis=0).astype(WIDE)
    scale1_all = lax.rsqrt(jnp.mean(hidden_all * hidden_all, axis=1, keepdims=True) + EPS)
    normed1 = (hidden_all * scale1_all * gain1[None, :]).astype(LOW)

    query_raw = mm(normed1, w_query_cols)
    kv_raw = mm(normed1, w_kv_cols)
    cos_q, sin_q = cosine[:, :, None, :], sine[:, :, None, :]
    query = rotate(query_raw.reshape(count, length, group, HEAD_DIM), cos_q, sin_q).astype(LOW)
    keys = rotate(kv_raw[:, :HEAD_DIM].reshape(count, length, HEAD_DIM), cosine, sine).astype(LOW)
    values = kv_raw[:, HEAD_DIM:].reshape(count, length, HEAD_DIM).astype(LOW)
    query = gate_cols.settle(query)
    gate_cols.trade(0)

    raw = jnp.einsum("bqgd,bkd->bgqk", query, keys, preferred_element_type=WIDE) * factor
    masked = jnp.where(allowed, raw, -1000000000.0)
    peak = jnp.max(masked, axis=-1, keepdims=True)
    expo = jnp.exp(masked - peak)
    total = jnp.sum(expo, axis=-1, keepdims=True)
    probs = expo / total
    probs_low = probs.astype(LOW)
    log_total = peak + jnp.log(total)
    attended = (
        jnp.einsum("bgqk,bkd->bqgd", probs_low, values, preferred_element_type=WIDE)
        .reshape(tokens, block)
        .astype(LOW)
    )
    attended = gate_cols.settle(attended, only=0)
    out_part = up_cols.settle(mm(attended, w_out).astype(LOW)).reshape(count, length, width)
    up_cols.trade(0)
    reduced = ring.scatter(
        [out_part[k] for k in range(count)], gate_cols.settle
    )
    outs = {
        "query": blank(w_query.shape),
        "key": blank(w_key.shape),
        "value": blank(w_value.shape),
        "out": blank((rows, width)),
        "gate": blank(w_gate.shape),
        "up": blank(w_up.shape),
        "down": blank(w_down.shape),
    }
    hidden = own_low.astype(WIDE)
    middle = hidden + reduced
    scale2 = lax.rsqrt(jnp.mean(middle * middle, axis=1, keepdims=True) + EPS)
    unit2 = middle * scale2
    normed2_own = (unit2 * gain2[None, :]).astype(LOW)
    normed2_blocks = ring.gather(normed2_own)
    (upstream_own,) = late([cotangent[0]], normed2_blocks[2])
    upstream_far = ring.swap(upstream_own, 2)
    normed2 = jnp.concatenate(normed2_blocks, axis=0)

    ff_own = w_down.shape[0]
    gate_cols.after(normed2_own)
    up_cols.after(normed2_own)
    w_gate_cols = gate_cols.whole()
    w_up_cols = up_cols.whole()
    gate = mm(normed2, w_gate_cols)
    upward = mm(normed2, w_up_cols)
    sigmoid_gate = jax.nn.sigmoid(gate)
    silu_gate = gate * sigmoid_gate
    inner = (silu_gate * upward).astype(LOW)
    (upstream_far,) = late([upstream_far], inner)
    upstream_all = jnp.concatenate(
        [
            upstream_own,
            ring.swap(upstream_own, 1),
            upstream_far,
            ring.swap(upstream_far, 1),
        ],
        axis=0,
    )

    def unpack(names, widths, n):
        def store(way, index, value):
            at = 0
            for name, cols in zip(names, widths):
                piece = value[:, at : at + cols]
                outs[name] = put(outs[name], piece, (way * reps + index) * n, 0)
                at += cols

        return store

    def first_blocks(parts):
        yield from ()
        return [part[0] for part in parts]

    grad_down = contract_rows(inner, upstream_all).astype(LOW)
    def chunk_of(value, axis):
        n = value.shape[axis] // (2 * reps)
        return lambda index: lax.dynamic_slice_in_dim(value, index * n, n, axis)

    n_down = ff_own // (2 * reps)
    flow.add(
        ring.ring_sum(
            chunk_of(grad_down[None], 1), first_blocks, unpack(["down"], [width], n_down)
        )
    )
    upstream_next, grad_down = tie(upstream_all, grad_down)
    inner_grad = contract_cols(upstream_next, w_down)
    gate_grad = (inner_grad * upward * sigmoid_gate * (1.0 + gate * (1.0 - sigmoid_gate))).astype(
        LOW
    )
    up_grad = (inner_grad * silu_gate).astype(LOW)
    gate_grad, up_grad = flow.pump(1, gate_grad, up_grad)

    n_rows = rows // (2 * reps)
    fulls = []
    for cols in (gate_grad, up_grad):
        full = contract_rows(normed2, cols).astype(LOW).reshape(count, rows, ff_own)
        full, gate_grad, up_grad = flow.pump(PUMPS[0], full, gate_grad, up_grad)
        fulls.append(chunk_of(full, 1))
    flow.add(
        ring.ring_sum(
            lambda index: jnp.concatenate([full(index) for full in fulls], axis=2),
            lambda v: ring.exchange(v, (0, ff_own, 2 * ff_own)),
            unpack(["gate", "up"], [count * ff_own] * 2, n_rows),
        )
    )

    back_part = contract_cols(gate_grad, w_gate_cols)
    back_part, up_grad = flow.pump(PUMPS[13], back_part, up_grad)
    back_part = (back_part + contract_cols(up_grad, w_up_cols)).astype(LOW)
    back_part = flow.pump(PUMPS[1], back_part).reshape(count, length, width)
    normed2_grad = ring.scatter([back_part[k] for k in range(count)], lambda v: flow.beside(PUMPS[2], v), flow)

    grad_mlp_gain = jnp.sum(normed2_grad * unit2, axis=0)
    middle_grad = cotangent[0].astype(WIDE) + norm_back(normed2_grad, gain2, unit2, scale2)
    middle_low = middle_grad.astype(LOW)
    flow.after(middle_low)
    branch_far = flow.beside(PUMPS[3], ring.swap(middle_low, 2))
    branch_grad = jnp.concatenate(
        [middle_low, ring.swap(middle_low, 1), branch_far, ring.swap(branch_far, 1)], axis=0
    )
    attended_grad = (
        contract_cols(branch_grad, w_out).astype(LOW).reshape(count, length, group, HEAD_DIM)
    )
    attended_grad = flow.pump(PUMPS[4], attended_grad)
    probs = jnp.exp(masked - log_total)
    probs_grad = jnp.einsum("bqgd,bkd->bgqk", attended_grad, values, preferred_element_type=WIDE)
    inner_sum = jnp.sum(probs * probs_grad, axis=-1, keepdims=True)
    score_grad = (probs * (probs_grad - inner_sum)).astype(LOW)
    score_grad = flow.pump(PUMPS[5], score_grad)
    query_part = (
        jnp.einsum("bgqk,bkd->bqgd", score_grad, keys, preferred_element_type=WIDE) * factor
    )
    key_part = jnp.einsum("bgqk,bqgd->bkd", score_grad, query, preferred_element_type=WIDE) * factor
    value_part = jnp.einsum(
        "bgqk,bqgd->bkd", probs.astype(LOW), attended_grad, preferred_element_type=WIDE
    )
    query_grad = rotate(query_part, cos_q, -sin_q).astype(LOW).reshape(tokens, block)
    key_grad = rotate(key_part, cosine, -sine).astype(LOW).reshape(tokens, HEAD_DIM)
    value_grad = value_part.astype(LOW).reshape(tokens, HEAD_DIM)
    qkv_grad = jnp.concatenate([query_grad, key_grad, value_grad], axis=1)
    qkv_grad = flow.pump(PUMPS[6], qkv_grad)

    grad_qkv = contract_rows(normed1, qkv_grad).astype(LOW)
    grad_out = contract_rows(attended, branch_grad).astype(LOW)
    grad_qkv, grad_out, qkv_grad = flow.pump(PUMPS[7], grad_qkv, grad_out, qkv_grad)
    qkv_cols = qkv_grad.shape[1]
    qkv_chunk = chunk_of(grad_qkv.reshape(count, rows, qkv_cols), 1)
    out_chunk = chunk_of(grad_out, 0)

    def attn_chunk(index):
        out = jnp.transpose(out_chunk(index).reshape(n_rows, count, rows), (1, 0, 2))
        return jnp.concatenate([qkv_chunk(index), out], axis=2)

    def attn_message(parts):
        moved = yield from ring.exchange([part[:, :, :qkv_cols] for part in parts], (0, qkv_cols))
        ends = (0, block, block + HEAD_DIM, qkv_cols)
        moved = [
            jnp.concatenate(
                [
                    whole[:, s * qkv_cols + a : s * qkv_cols + b]
                    for a, b in zip(ends, ends[1:])
                    for s in range(count)
                ],
                axis=1,
            )
            for whole in moved
        ]
        still = [
            jnp.transpose(part[:, :, qkv_cols:], (1, 0, 2)).reshape(n_rows, width)
            for part in parts
        ]
        return [jnp.concatenate(both, axis=1) for both in zip(moved, still)]

    flow.add(
        ring.ring_sum(
            attn_chunk,
            attn_message,
            unpack(
                ["query", "key", "value", "out"],
                [w_query.shape[1], w_key.shape[1], w_value.shape[1], width],
                n_rows,
            ),
        )
    )

    qkv_grad = flow.pump(PUMPS[12], qkv_grad)
    back_part = (
        contract_cols(qkv_grad[:, :block], w_query_cols)
        + contract_cols(qkv_grad[:, block:], w_kv_cols)
    ).astype(LOW)
    back_part = flow.pump(1, back_part).reshape(count, length, width)
    normed1_grad = ring.scatter([back_part[k] for k in range(count)], lambda v: flow.beside(PUMPS[8], v), flow)
    scale1 = lax.rsqrt(jnp.mean(hidden * hidden, axis=1, keepdims=True) + EPS)
    unit1 = hidden * scale1
    grad_attn_gain = jnp.sum(normed1_grad * unit1, axis=0)
    input_grad = middle_grad + norm_back(normed1_grad, gain1, unit1, scale1)
    def gain_sum(both):
        k = 1
        while k < count:
            (got,) = yield [ring.swap(both, k)], [both]
            both = both + got
            k *= 2
        both = lax.dynamic_slice_in_dim(both, ring.shard * rows, rows, 1)
        k = 1
        while k < reps:
            (got,) = yield [ring.pair(both, k)], [both]
            both = both + got
            k *= 2
        outs["gains"] = both

    flow.add(gain_sum(jnp.stack([grad_attn_gain, grad_mlp_gain])))
    (inner,) = late([inner], input_grad)

    down_part = mm(inner, w_down).astype(LOW)
    down_part = flow.pump(PUMPS[10], down_part).reshape(count, length, width)
    layer_out = (
        middle + ring.scatter([down_part[k] for k in range(count)], lambda v: flow.beside(PUMPS[11], v), flow)
    ).astype(LOW)

    flow.finish()
    mine = outs["gains"]

    return (
        layer_out[None],
        input_grad[None],
        mine[0],
        outs["query"],
        outs["key"],
        outs["value"],
        outs["out"],
        mine[1],
        outs["gate"],
        outs["up"],
        outs["down"],
    )


def solution(mesh):
    both = ("shard", "rep")
    row, vec = P("shard", None), P("shard")
    act = P(both, None, None)
    in_specs = (act, P(both, None), act, vec, row, row, row, row, vec, row, row, row)
    out_specs = (act, act, vec, row, row, row, row, vec, row, row, row)

    def body(*args):
        return shards(mesh, *args)

    return jax.shard_map(
        body, mesh=mesh, in_specs=in_specs, out_specs=out_specs, check_vma=False
    )
```
